256 devices in a mesh: blk: 32 (over x, y, core), sub: 8 (over z).
Axes of the slice: x: 4, y: 4, z: 8, core: 2. Of those that a mesh axis runs over, the one named last changes fastest.
Arguments:
- adjoint: float32 [6, 32, 32, 64, 128], P(None, 'blk', 'sub'), may hold values from -6 to 6
- source: float32 [6, 32, 32, 64, 128], P(None, 'blk', 'sub'), may hold values from -6 to 6
- cell_coef: float32 [4, 32, 32, 64, 128], P(None, 'blk', 'sub'), may hold values from 0.5 to 2
- flux_jacobian: float32 [32, 3, 2, 6, 6], P('blk'), may hold values from -2.5 to 2.5
- fringe_dest: int32 [1048576, 1], P(('blk', 'sub')), may hold values from 0 to 31; in each aligned block of 4096 rows (0 to 4095, 4096 to 8191, ...) at most 256 rows name the same one
- fringe_cell: int32 [1048576], P(('blk', 'sub')), may hold values from 0 to 32767
- fringe_base: int32 [1048576], P(('blk', 'sub')), may hold values from 0 to 24446, as said below
- fringe_frac: float32 [3, 1048576], P(None, ('blk', 'sub')), may hold values from 0 to 1
Outputs:
- adjoint_residual: float32 [6, 32, 32, 64, 128], P(None, 'blk', 'sub')
The draws below stay inside these ranges and needn't reach their ends.
Inputs may be any that keep to these rules, and one draw needn't show every extreme that they name: `fringe_dest`: in each aligned block of 4096 rows (the records of one device), no blk index is named by more than 256 rows. `fringe_base`: A donor base cell (n, i, j, k) in the local numbering always has i < 3, j < 63 and k < 127, so all eight corners lie on the record's own device and block.
All inputs are finite; a program needn't handle non-finite values.
Results may differ from the reference program's by a relative error of at most 0.0001.
Values sent between devices are 32-bit elements; how exact they have to be, the bound alone decides.
A program may use at most 128 MiB of HBM per device.

```python
import math
import jax
import jax.numpy as jnp
import numpy as np
from jax import lax

NVAR = 6
NB_DEV = 1
ID = 4
J = 64
K = 128
BLOCKS = 32
I = 32
CELLS_DEV = 32768
CAP = 256
R = 4096
RECS = 1048576
N_BLK = 32
N_SUB = 8


def draw_fringe_base(key, part):
    key_block, key_first, key_second, key_third = jax.random.split(key, 4)
    block_pick = jax.random.randint(key_block, (RECS,), 0, NB_DEV)
    first_pick = jax.random.randint(key_first, (RECS,), 0, ID - 1)
    second_pick = jax.random.randint(key_second, (RECS,), 0, J - 1)
    third_pick = jax.random.randint(key_third, (RECS,), 0, K - 1)
    positions = jnp.arange(RECS, dtype=jnp.int32)
    block_pick = jnp.where(positions == 0, NB_DEV - 1, jnp.where(positions == 1, 0, block_pick))
    first_pick = jnp.where(positions == 0, ID - 2, jnp.where(positions == 1, 0, first_pick))
    second_pick = jnp.where(positions == 0, J - 2, jnp.where(positions == 1, 0, second_pick))
    third_pick = jnp.where(positions == 0, K - 2, jnp.where(positions == 1, 0, third_pick))
    flat_index = ((block_pick * ID + first_pick) * J + second_pick) * K + third_pick
    return flat_index.astype(jnp.int32)


def plant(entries, rng, smallest, largest):
    extent = entries.shape
    spot = [jax.random.randint(jax.random.fold_in(rng, axis), (), 0, extent[axis]) for axis in range(len(extent))]
    entries = entries.at[tuple(spot)].set(smallest)
    longest = extent.index(max(extent))
    spot[longest] = (spot[longest] + 1) % extent[longest]
    return entries.at[tuple(spot)].set(largest)


def shard_levels(key, extent, cuts, low, top_value):
    gain, own = 1.0, jax.random.fold_in(key, 6)
    for dim, blocks in cuts:
        steps = jnp.exp(jax.random.uniform(jax.random.fold_in(own, dim), (blocks,), jnp.float32, low / len(cuts), top_value / len(cuts)))
        gain = gain * jnp.repeat(steps, extent[dim] // blocks).reshape([-1 if axis == dim else 1 for axis in range(len(extent))])
    return gain


def assign_block(key, own, number, rows, amount, top, reach, skew):
    ranking = jax.random.permutation(key, amount)
    crowded, common = portions_of(amount, rows * top, reach, skew, True), portions_of(amount, rows * top, reach, skew, False)
    places = jnp.arange(amount)

    def named(sizes, turn):
        used = int((sizes > 0).sum())
        fixed = max(1, used // 4)
        passed = fixed + (places - fixed + turn * (used - fixed)) % max(1, amount - fixed)
        return jnp.zeros((amount,), jnp.int32).at[ranking[jnp.where(places < fixed, places, passed)]].set(jnp.asarray(sizes, jnp.int32))

    sizes = jnp.where(number % 4 == 0, named(crowded, number // 4), named(common, number - number // 4 - 1))
    mixed = jax.random.permutation(jax.random.fold_in(own, 3), amount)
    donor, receiver = mixed[0:amount // 2 * 2:2], mixed[1:amount // 2 * 2:2]
    room = jnp.minimum(sizes[donor] - 1, reach - sizes[receiver]) // 2
    room = jnp.where((donor == ranking[0]) | (receiver == ranking[0]) | (sizes[receiver] == 0), 0, jnp.maximum(room, 0))
    passed = jax.random.randint(jax.random.fold_in(own, 4), (amount // 2,), 0, 1 << 20) % (room + 1)
    sizes = sizes.at[donor].add(-passed).at[receiver].add(passed)
    members = jnp.searchsorted(jnp.cumsum(sizes), jnp.arange(rows * top), side="right").astype(jnp.int32)
    grid = members.reshape(top, rows).T
    grid = grid[jax.random.permutation(jax.random.fold_in(own, 1), rows)]
    turn = jax.random.randint(jax.random.fold_in(own, 2), (rows, 1), 0, top)
    return jnp.take_along_axis(grid, (jnp.arange(top)[None, :] + turn) % top, axis=1)


def portions_of(amount, total, reach, skew, full):
    weights = [(1 << 20) // math.isqrt(rank ** skew) + 1 for rank in range(1, amount + 1)]
    largest = reach if full else min(reach, max(-(-total // amount), total * weights[0] // sum(weights)))
    least = 1 if total - largest >= amount - 1 else 0
    given, spare = [largest] + [least] * (amount - 1), total - largest - least * (amount - 1)
    while spare > 0:
        movable = [i for i in range(1, amount) if given[i] < largest] or [i for i in range(1, amount) if given[i] < reach]
        pool, left = sum([weights[i] for i in movable]), spare
        for i in movable:
            extra = min(reach - given[i], max(1, left * weights[i] // pool), spare)
            given[i] = given[i] + extra
            spare = spare - extra
    return np.array(given)


def scatter_about(stream_key, extent, deviation, bound, cuts=(), kind=jnp.bfloat16):
    values = deviation * jax.random.normal(stream_key, extent, jnp.float32)
    if cuts:
        values = values * shard_levels(stream_key, extent, cuts, -0.22, 0.18)
    return jnp.clip(values, -bound, bound).astype(kind)


def setup_inputs(seed: int = 0) -> dict:
    streams_of = jax.random.split(jax.random.key(seed), 9)
    adjoint = scatter_about(streams_of[0], (NVAR, BLOCKS, I, J, K), 1.0, 6.0, ((1, 32), (2, 8)), jnp.float32)
    source = scatter_about(streams_of[1], (NVAR, BLOCKS, I, J, K), 1.0, 6.0, ((1, 32), (2, 8)), jnp.float32)
    cell_coef = jnp.clip(jnp.exp(math.log(2.0) - 1.3862944 * jax.random.uniform(streams_of[2], (4, BLOCKS, I, J, K), jnp.float32) ** shard_levels(streams_of[2], (4, BLOCKS, I, J, K), ((1, 32), (2, 8)), -0.2, 0.2)), 0.5, 2.0)
    flux_jacobian = scatter_about(streams_of[3], (BLOCKS, 3, 2, NVAR, NVAR), NVAR ** -0.5, 2.5, ((0, 32),), jnp.float32)
    fringe_dest_keys = jax.random.split(jax.random.fold_in(streams_of[4], 1), RECS // R)
    fringe_dest_turns = jax.random.permutation(jax.random.fold_in(streams_of[4], 3), RECS // R)
    fringe_dest = jax.vmap(lambda own, number: assign_block(jax.random.fold_in(streams_of[4], 2), own, number, R, N_BLK, 1, CAP, 2))(fringe_dest_keys, fringe_dest_turns).reshape((RECS, 1))
    fringe_cell = plant(jax.random.randint(streams_of[5], (RECS,), 0, CELLS_DEV), jax.random.fold_in(streams_of[5], 1), 0, CELLS_DEV - 1).astype(jnp.int32)
    fringe_base = draw_fringe_base(jax.random.fold_in(streams_of[8], 71), 0)
    fringe_frac = jnp.clip(1.0 * jax.random.uniform(streams_of[7], (3, RECS), jnp.float32) ** shard_levels(streams_of[7], (3, RECS), ((1, 256),), -0.2, 0.2), 0.0, 1.0)
    return dict(adjoint=adjoint, source=source, cell_coef=cell_coef, flux_jacobian=flux_jacobian, fringe_dest=fringe_dest, fringe_cell=fringe_cell, fringe_base=fringe_base, fringe_frac=fringe_frac)


def corner_weights(fractions, row_stride, col_stride):
    listing = []
    for step_i in range(2):
        weight_i = fractions[0] if step_i else 1.0 - fractions[0]
        for step_j in range(2):
            weight_j = fractions[1] if step_j else 1.0 - fractions[1]
            for step_k in range(2):
                weight_k = fractions[2] if step_k else 1.0 - fractions[2]
                offset = step_i * row_stride + step_j * col_stride + step_k
                listing.append((offset, weight_i * weight_j * weight_k))
    return listing


def to_slabs(grid_field):
    shaped = grid_field.reshape(NVAR, N_BLK, NB_DEV, N_SUB, ID, J, K)
    shaped = shaped.transpose(0, 1, 3, 2, 4, 5, 6)
    return shaped.reshape(NVAR, N_BLK * N_SUB * CELLS_DEV)


def from_slabs(flat_field):
    shaped = flat_field.reshape(NVAR, N_BLK, N_SUB, NB_DEV, ID, J, K)
    shaped = shaped.transpose(0, 1, 3, 2, 4, 5, 6)
    return shaped.reshape(NVAR, BLOCKS, I, J, K)


def shift_next(grid_field, grid_axis):
    length = grid_field.shape[grid_axis]
    sliced = lax.slice_in_dim(grid_field, 1, length, axis=grid_axis)
    widths = [(0, 0)] * grid_field.ndim
    widths[grid_axis] = (0, 1)
    return jnp.pad(sliced, widths)


def shift_prev(grid_field, grid_axis):
    length = grid_field.shape[grid_axis]
    sliced = lax.slice_in_dim(grid_field, 0, length - 1, axis=grid_axis)
    widths = [(0, 0)] * grid_field.ndim
    widths[grid_axis] = (1, 0)
    return jnp.pad(sliced, widths)


def transposed_sweep(grid_field, cell_coef, flux_jacobian):
    running = cell_coef[0] * grid_field
    for direction in range(3):
        upper_term = jnp.einsum("bve,vbijk->ebijk", flux_jacobian[:, direction, 0], grid_field, precision=lax.Precision.HIGHEST)
        lower_term = jnp.einsum("bve,vbijk->ebijk", flux_jacobian[:, direction, 1], grid_field, precision=lax.Precision.HIGHEST)
        from_next = shift_next(upper_term, 2 + direction)
        from_prev = shift_prev(lower_term, 2 + direction)
        running = running + cell_coef[direction + 1] * (from_next + from_prev)
    return running


def reference(adjoint, source, cell_coef, flux_jacobian, fringe_dest, fringe_cell, fringe_base, fringe_frac):
    adj_flat = to_slabs(adjoint)
    owner = jnp.arange(RECS, dtype=jnp.int32) // R
    sub_index = owner % N_SUB
    anchor = owner * CELLS_DEV
    weights = corner_weights(fringe_frac, J * K, K)
    interp_value = jnp.zeros((NVAR, RECS), jnp.float32)
    for offset, weight in weights:
        interp_value = interp_value + weight * adj_flat[:, anchor + fringe_base + offset]
    target = (fringe_dest[:, 0] * N_SUB + sub_index) * CELLS_DEV + fringe_cell
    merged = adj_flat.at[:, target].add(interp_value)
    image = transposed_sweep(from_slabs(merged), cell_coef, flux_jacobian)
    residual = source - image
    res_flat = to_slabs(residual)
    at_receivers = res_flat[:, target]
    result = res_flat
    for offset, weight in weights:
        result = result.at[:, anchor + fringe_base + offset].add(weight * at_receivers)
    return from_slabs(result)
```

```python
import functools

import jax
import jax.numpy as jnp
from jax import lax
from jax.experimental import pallas as pl
from jax.experimental.pallas import tpu as pltpu
from jax.sharding import PartitionSpec as P

NV, NI, NJ, NK = 6, 4, 64, 128
NR = NI * NJ
R = 4096
G = 32
CAP = 256
F32, BF16, I32 = jnp.float32, jnp.bfloat16, jnp.int32
VMEM = pl.BlockSpec(memory_space=pltpu.VMEM)
NT = (((1,), (1,)), ((), ()))


def split(x):
    hi = x.astype(BF16)
    return hi, (x - hi.astype(F32)).astype(BF16)


def rows(n, m):
    return lax.broadcasted_iota(I32, (n, m), 0)


def corner_rows(base, frac, n):
    i0, j0 = base >> 13, (base >> 7) & 63
    f0, f1 = frac[0:1], frac[1:2]
    jj = rows(NJ, n)
    wj = jnp.where(jj == j0, 1.0 - f1, jnp.where(jj == j0 + 1, f1, 0.0))
    parts = []
    for i in range(NI):
        wi = jnp.where(i0 == i, 1.0 - f0, jnp.where(i0 == i - 1, f0, 0.0))
        parts.append(wj * wi)
    return jnp.concatenate(parts, axis=0)


def corner_cols(base, frac, n):
    k0, f2 = base & 127, frac[2:3]
    kk = rows(NK, n)
    return jnp.where(kk == k0, 1.0 - f2, jnp.where(kk == k0 + 1, f2, 0.0))


def transposed_field(field, ft_ref, copies):
    for v in range(NV):
        hi, lo = split(field(v).T)
        at = pl.ds(v * NK, NK)
        for c, part in enumerate((hi, lo, hi)[:copies]):
            ft_ref[at, c * NR : (c + 1) * NR] = part


def donor_kernel(adj, dest, cell, base, frac, send, rank, ft, vals, pick, *, n, m):
    transposed_field(lambda v: adj[v], ft, 3)

    tri = (rows(256, 256) < lax.broadcasted_iota(I32, (256, 256), 1)).astype(F32).astype(BF16)
    carry = jnp.zeros((G, 1), F32)
    for c in range(R // 256):
        at = slice(c * 256, (c + 1) * 256)
        hot = (rows(G, 256) == dest[:, at]).astype(F32)
        before = jnp.dot(hot.astype(BF16), tri, preferred_element_type=F32) + carry
        carry = carry + jnp.sum(hot, axis=1, keepdims=True)
        rank[:, at] = jnp.sum(hot * before, axis=0, keepdims=True).astype(I32)

    @pl.loop(0, R // n)
    def _(c):
        at = pl.ds(pl.multiple_of(c * n, n), n)
        b, f = base[:, at], frac[:, at]
        hi, lo = split(corner_rows(b, f, n))
        t = jnp.dot(ft[...], jnp.concatenate([hi, hi, lo], axis=0), preferred_element_type=F32)
        wk = corner_cols(b, f, n)
        out = [jnp.sum(t[v * NK : (v + 1) * NK] * wk, axis=0, keepdims=True) for v in range(NV)]
        out += [cell[:, at].astype(F32), jnp.zeros((1, n), F32)]
        vals[:, at] = jnp.concatenate(out, axis=0)

    @pl.loop(0, R // m)
    def _(c):
        at = pl.ds(pl.multiple_of(c * m, m), m)
        hi, lo = split(vals[:, at])
        both = jnp.concatenate([hi.astype(F32), lo.astype(F32)], axis=0)
        to = dest[:, at]
        for d in range(G):
            pick[d * 16 : (d + 1) * 16] = jnp.where(to == d, both, 0.0).astype(BF16)
        place = (rows(CAP, m) == rank[:, at]).astype(F32).astype(BF16)
        t = lax.dot_general(pick[...], place, NT, preferred_element_type=F32)
        t = t.reshape(G, 16, CAP)
        t = t[:, :8] + t[:, 8:]

        @pl.when(c == 0)
        def _():
            send[...] = t

        @pl.when(c > 0)
        def _():
            send[...] += t


def scatter_kernel(adj, got, psi, acc, *, u):
    acc[...] = jnp.zeros_like(acc)

    @pl.loop(0, G // u)
    def _(c):
        left, right = [], [[] for _ in range(NV)]
        for p in range(u):
            g = got[c * u + p]
            cell = g[6:7].astype(I32)
            oi = (rows(NR, CAP) == cell >> 7).astype(F32).astype(BF16)
            ok = rows(NK, CAP) == (cell & 127)
            hi, lo = split(g)
            hi, lo = hi.astype(F32), lo.astype(F32)
            left += [oi, oi]
            for v in range(NV):
                right[v] += [
                    jnp.where(ok, hi[v : v + 1], 0.0).astype(BF16),
                    jnp.where(ok, lo[v : v + 1], 0.0).astype(BF16),
                ]
        left = jnp.concatenate(left, axis=1)
        right = jnp.concatenate([jnp.concatenate(r, axis=1) for r in right], axis=0)
        acc[...] += lax.dot_general(left, right, NT, preferred_element_type=F32)

    for v in range(NV):
        psi[v] = adj[v] + acc[:, v * NK : (v + 1) * NK]


def stencil_kernel(psi, low, high, source, coef, jac, got, res, back, pad, ft, *, tj):
    for v in range(NV):
        pad[v, 0:NJ] = low[v]
        pad[v, NJ : NJ + NR] = psi[v]
        pad[v, NJ + NR :] = high[v]
    kk = lax.broadcasted_iota(I32, (tj, NK), 1)

    @pl.loop(0, NR // tj)
    def _(c):
        r0 = pl.multiple_of(c * tj, tj)
        jj = (rows(tj, NK) + r0) & (NJ - 1)
        total = [[None] * NV for _ in range(3)]
        mid = [pad[v, pl.ds(r0 + NJ, tj)] for v in range(NV)]

        def add(d, s, v, x):
            for e in range(NV):
                term = jac[((d * 2 + s) * NV + v) * NV + e] * x
                total[d][e] = term if total[d][e] is None else total[d][e] + term

        for v in range(NV):
            add(0, 0, v, pad[v, pl.ds(r0 + 2 * NJ, tj)])
            add(0, 1, v, pad[v, pl.ds(r0, tj)])
            add(1, 0, v, jnp.where(jj == NJ - 1, 0.0, pad[v, pl.ds(r0 + NJ + 1, tj)]))
            add(1, 1, v, jnp.where(jj == 0, 0.0, pad[v, pl.ds(r0 + NJ - 1, tj)]))
            add(2, 0, v, jnp.where(kk == NK - 1, 0.0, pltpu.roll(mid[v], NK - 1, 1)))
            add(2, 1, v, jnp.where(kk == 0, 0.0, pltpu.roll(mid[v], 1, 1)))
        at = pl.ds(r0, tj)
        for e in range(NV):
            image = coef[0, at] * mid[e]
            for d in range(3):
                image += coef[d + 1, at] * total[d][e]
            res[e, at] = source[e, at] - image

    transposed_field(lambda v: res[v], ft, 2)

    @pl.loop(0, G)
    def _(s):
        cell = got[s, 6:7].astype(I32)
        oi = (rows(NR, CAP) == cell >> 7).astype(F32).astype(BF16)
        ok = rows(NK, CAP) == (cell & 127)
        t = jnp.dot(ft[...], jnp.concatenate([oi, oi], axis=0), preferred_element_type=F32)
        out = [
            jnp.sum(jnp.where(ok, t[v * NK : (v + 1) * NK], 0.0), axis=0, keepdims=True)
            for v in range(NV)
        ]
        back[s] = jnp.concatenate(out + [jnp.zeros((2, CAP), F32)], axis=0)


def finish_kernel(res, back, rank, dest, base, frac, out, parts, acc, *, n):
    acc[...] = jnp.zeros_like(acc)
    for d in range(G):
        hi, lo = split(back[d])
        parts[d * 16 : (d + 1) * 16] = jnp.concatenate([hi.astype(F32), lo.astype(F32)], axis=0).astype(BF16)

    @pl.loop(0, R // n)
    def _(c):
        at = pl.ds(pl.multiple_of(c * n, n), n)
        place = (rows(CAP, n) == rank[:, at]).astype(F32).astype(BF16)
        t = jnp.dot(parts[...], place, preferred_element_type=F32)
        to = dest[:, at]
        both = jnp.zeros((16, n), F32)
        for d in range(G):
            both = jnp.where(to == d, t[d * 16 : (d + 1) * 16], both)
        value = both[:8] + both[8:]
        b, f = base[:, at], frac[:, at]
        ah, al = split(corner_rows(b, f, n))
        wk = corner_cols(b, f, n)
        left = jnp.concatenate([ah, ah, al], axis=1)
        right = []
        for v in range(NV):
            hi, lo = split(wk * value[v : v + 1])
            right.append(jnp.concatenate([hi, lo, hi], axis=1))
        right = jnp.concatenate(right, axis=0)
        acc[...] += lax.dot_general(left, right, NT, preferred_element_type=F32)

    for v in range(NV):
        out[v] = res[v] + acc[:, v * NK : (v + 1) * NK]


def params():
    return pltpu.CompilerParams(vmem_limit_bytes=48 << 20)


def donor(adj, dest, cell, base, frac, n=512, m=1024):
    return pl.pallas_call(
        functools.partial(donor_kernel, n=n, m=m),
        out_shape=(jax.ShapeDtypeStruct((G, 8, CAP), F32), jax.ShapeDtypeStruct((1, R), I32)),
        in_specs=[VMEM] * 5,
        out_specs=(VMEM, VMEM),
        scratch_shapes=[
            pltpu.VMEM((NV * NK, 3 * NR), BF16),
            pltpu.VMEM((8, R), F32),
            pltpu.VMEM((G * 16, m), BF16),
        ],
        compiler_params=params(),
        name="donor",
    )(adj, dest, cell, base, frac)


def scatter(adj, got, u=2):
    return pl.pallas_call(
        functools.partial(scatter_kernel, u=u),
        out_shape=jax.ShapeDtypeStruct((NV, NR, NK), F32),
        in_specs=[VMEM] * 2,
        out_specs=VMEM,
        scratch_shapes=[pltpu.VMEM((NR, NV * NK), F32)],
        compiler_params=params(),
        name="scatter",
    )(adj, got)


def stencil(psi, low, high, source, coef, jac, got, tj=16):
    return pl.pallas_call(
        functools.partial(stencil_kernel, tj=tj),
        out_shape=(jax.ShapeDtypeStruct((NV, NR, NK), F32), jax.ShapeDtypeStruct((G, 8, CAP), F32)),
        in_specs=[VMEM] * 5 + [pl.BlockSpec(memory_space=pltpu.SMEM), VMEM],
        out_specs=(VMEM, VMEM),
        scratch_shapes=[
            pltpu.VMEM((NV, NR + 2 * NJ, NK), F32),
            pltpu.VMEM((NV * NK, 2 * NR), BF16),
        ],
        compiler_params=params(),
        name="stencil",
    )(psi, low, high, source, coef, jac, got)


def finish(res, back, rank, dest, base, frac, n=512):
    return pl.pallas_call(
        functools.partial(finish_kernel, n=n),
        out_shape=jax.ShapeDtypeStruct((NV, NR, NK), F32),
        in_specs=[VMEM] * 6,
        out_specs=VMEM,
        scratch_shapes=[
            pltpu.VMEM((G * 16, CAP), BF16),
            pltpu.VMEM((NR, NV * NK), F32),
        ],
        compiler_params=params(),
        name="finish",
    )(res, back, rank, dest, base, frac)


def per_device(adjoint, source, cell_coef, flux_jacobian, fringe_dest, fringe_cell, fringe_base, fringe_frac):
    adj = adjoint.reshape(NV, NR, NK)
    src = source.reshape(NV, NR, NK)
    coef = cell_coef.reshape(4, NR, NK)
    jac = flux_jacobian.reshape(3 * 2 * NV * NV)
    dest = fringe_dest.reshape(1, R)
    cell = fringe_cell.reshape(1, R)
    base = fringe_base.reshape(1, R)

    send, rank = donor(adj, dest, cell, base, fringe_frac)
    got = lax.all_to_all(send, "blk", split_axis=0, concat_axis=0, tiled=True)
    psi = scatter(adj, got)
    count = lax.axis_size("sub")
    up = [(i, i + 1) for i in range(count - 1)]
    low = lax.ppermute(psi[:, NR - NJ :], "sub", up)
    high = lax.ppermute(psi[:, :NJ], "sub", [(t, s) for s, t in up])
    res, back = stencil(psi, low, high, src, coef, jac, got)
    back = lax.all_to_all(back, "blk", split_axis=0, concat_axis=0, tiled=True)
    out = finish(res, back, rank, dest, base, fringe_frac)
    return out.reshape(adjoint.shape)


def solution(mesh):
    return jax.shard_map(
        per_device,
        mesh=mesh,
        in_specs=(
            P(None, "blk", "sub", None, None),
            P(None, "blk", "sub", None, None),
            P(None, "blk", "sub", None, None),
            P("blk", None, None, None, None),
            P(("blk", "sub"), None),
            P(("blk", "sub")),
            P(("blk", "sub")),
            P(None, ("blk", "sub")),
        ),
        out_specs=P(None, "blk", "sub", None, None),
        check_vma=False,
    )
```

```python
import functools

import jax
import jax.numpy as jnp
from jax import lax
from jax.experimental import pallas as pl
from jax.experimental.pallas import tpu as pltpu
from jax.sharding import PartitionSpec as P

NV, NI, NJ, NK = 6, 4, 64, 128
NR = NI * NJ
R = 4096
G = 32
CAP = 256
F32, BF16, I32 = jnp.float32, jnp.bfloat16, jnp.int32
VMEM = pl.BlockSpec(memory_space=pltpu.VMEM)
MESH = pl.DeviceIdType.MESH
NT = (((1,), (1,)), ((), ()))


def split(x):
    hi = x.astype(BF16)
    return hi, (x - hi.astype(F32)).astype(BF16)


def rows(n, m):
    return lax.broadcasted_iota(I32, (n, m), 0)


def corner_rows(base, frac, n):
    i0, j0 = base >> 13, (base >> 7) & 63
    f0, f1 = frac[0:1], frac[1:2]
    jj = rows(NJ, n)
    wj = jnp.where(jj == j0, 1.0 - f1, jnp.where(jj == j0 + 1, f1, 0.0))
    parts = []
    for i in range(NI):
        wi = jnp.where(i0 == i, 1.0 - f0, jnp.where(i0 == i - 1, f0, 0.0))
        parts.append(wj * wi)
    return jnp.concatenate(parts, axis=0)


def corner_cols(base, frac, n):
    k0, f2 = base & 127, frac[2:3]
    kk = rows(NK, n)
    return jnp.where(kk == k0, 1.0 - f2, jnp.where(kk == k0 + 1, f2, 0.0))


def transposed_field(field, ft_ref, copies):
    for v in range(NV):
        hi, lo = split(field(v).T)
        at = pl.ds(v * NK, NK)
        for c, part in enumerate((hi, lo, hi)[:copies]):
            ft_ref[at, c * NR : (c + 1) * NR] = part


def one_hot(index, n):
    return (rows(n, index.shape[1]) == index).astype(F32).astype(BF16)


def chunk(c, n):
    return pl.ds(pl.multiple_of(c * n, n), n)


def find_ranks(dest, rank):
    tri = (rows(256, 256) < lax.broadcasted_iota(I32, (256, 256), 1)).astype(F32).astype(BF16)

    def step(c, carry):
        at = chunk(c, 256)
        hot = (rows(G, 256) == dest[:, at]).astype(F32)
        before = jnp.dot(hot.astype(BF16), tri, preferred_element_type=F32) + carry
        rank[:, at] = jnp.sum(hot * before, axis=0, keepdims=True).astype(I32)
        return carry + jnp.sum(hot, axis=1, keepdims=True)

    lax.fori_loop(0, R // 256, step, jnp.zeros((G, 1), F32), unroll=True)


def interpolate(ft, cell, base, frac, vals, n, unroll):
    def step(c, _):
        at = chunk(c, n)
        b, f = base[:, at], frac[:, at]
        hi, lo = split(corner_rows(b, f, n))
        t = jnp.dot(ft[...], jnp.concatenate([hi, hi, lo], axis=0), preferred_element_type=F32)
        wk = corner_cols(b, f, n)
        out = [jnp.sum(t[v * NK : (v + 1) * NK] * wk, axis=0, keepdims=True) for v in range(NV)]
        out += [cell[:, at].astype(F32), jnp.zeros((1, n), F32)]
        vals[:, at] = jnp.concatenate(out, axis=0)
        return 0

    lax.fori_loop(0, R // n, step, 0, unroll=unroll)


def pack(vals, dest, rank, pick, send):
    hi, lo = split(vals[...])
    both = jnp.concatenate([hi.astype(F32), lo.astype(F32)], axis=0)
    to = jnp.broadcast_to(dest[...], (16, R))

    def step(d, _):
        pick[pl.ds(pl.multiple_of(d * 16, 16), 16)] = jnp.where(to == d, both, 0.0).astype(BF16)
        return 0

    lax.fori_loop(0, G, step, 0, unroll=4)
    t = lax.dot_general(pick[...], one_hot(rank[...], CAP), NT, preferred_element_type=F32)
    t = t.reshape(G, 16, CAP)
    send[...] = t[:, :8] + t[:, 8:]


def add_received(got, acc, first, count, u):
    def step(c, _):
        left, right = [], [[] for _ in range(count)]
        for p in range(u):
            g = got[c * u + p]
            cell = g[6:7].astype(I32)
            oi = one_hot(cell >> 7, NR)
            ok = one_hot(cell & 127, NK)
            hi, lo = split(g)
            left += [oi, oi]
            for v in range(count):
                at = slice(first + v, first + v + 1)
                right[v] += [ok * hi[at], ok * lo[at]]
        left = jnp.concatenate(left, axis=1)
        right = jnp.concatenate([jnp.concatenate(r, axis=1) for r in right], axis=0)
        acc[...] += lax.dot_general(left, right, NT, preferred_element_type=F32)
        return 0

    acc[...] = jnp.zeros_like(acc)
    lax.fori_loop(0, G // u, step, 0)


def stencil_rows(pad, source, coef, jac, res, first, count, tj):
    kk = lax.broadcasted_iota(I32, (tj, NK), 1)

    def step(c, _):
        r0 = pl.multiple_of(first + c * tj, tj)
        jj = (rows(tj, NK) + r0) & (NJ - 1)
        total = [[None] * NV for _ in range(3)]
        mid = [pad[v, pl.ds(r0 + NJ, tj)] for v in range(NV)]

        def add(d, s, v, x):
            for e in range(NV):
                term = jac[((d * 2 + s) * NV + v) * NV + e] * x
                total[d][e] = term if total[d][e] is None else total[d][e] + term

        for v in range(NV):
            add(0, 0, v, pad[v, pl.ds(r0 + 2 * NJ, tj)])
            add(0, 1, v, pad[v, pl.ds(r0, tj)])
            add(1, 0, v, jnp.where(jj == NJ - 1, 0.0, pad[v, pl.ds(r0 + NJ + 1, tj)]))
            add(1, 1, v, jnp.where(jj == 0, 0.0, pad[v, pl.ds(r0 + NJ - 1, tj)]))
            add(2, 0, v, jnp.where(kk == NK - 1, 0.0, pltpu.roll(mid[v], NK - 1, 1)))
            add(2, 1, v, jnp.where(kk == 0, 0.0, pltpu.roll(mid[v], 1, 1)))
        at = pl.ds(r0, tj)
        for e in range(NV):
            image = coef[0, at] * mid[e]
            for d in range(3):
                image += coef[d + 1, at] * total[d][e]
            res[e, at] = source[e, at] - image
        return 0

    lax.fori_loop(0, count // tj, step, 0)


def unpack_and_add(ret, rank, dest, base, frac, parts, acc, n, unroll):
    for d in range(G):
        hi, lo = split(ret[d])
        parts[d * 16 : (d + 1) * 16] = jnp.concatenate([hi.astype(F32), lo.astype(F32)], axis=0).astype(BF16)

    def step(c, _):
        at = chunk(c, n)
        t = jnp.dot(parts[...], one_hot(rank[:, at], CAP), preferred_element_type=F32)
        to = jnp.broadcast_to(dest[:, at], (16, n))
        both = jnp.zeros((16, n), F32)
        for d in range(G):
            both = jnp.where(to == d, t[d * 16 : (d + 1) * 16], both)
        value = both[:8] + both[8:]
        b, f = base[:, at], frac[:, at]
        ah, al = split(corner_rows(b, f, n))
        wk = corner_cols(b, f, n)
        left = jnp.concatenate([ah, ah, al], axis=1)
        right = []
        for v in range(NV):
            hi, lo = split(wk * value[v : v + 1])
            right.append(jnp.concatenate([hi, lo, hi], axis=1))
        right = jnp.concatenate(right, axis=0)
        acc[...] += lax.dot_general(left, right, NT, preferred_element_type=F32)
        return 0

    acc[...] = jnp.zeros_like(acc)
    lax.fori_loop(0, R // n, step, 0, unroll=unroll)


VG = 2


def kernel(
    adj_h, src_h, coef_h, dest_h, cell_h, base_h, frac_h, jac, out,
    src, coef, dest, cell, base, frac, rank, ft, vals, pick, send, got, back, ret, pad, acc, sums, res, parts,
    load_sem, send1, recv1, send2, recv2, halo_send, halo_recv,
):
    me, z = lax.axis_index("blk"), lax.axis_index("sub")
    nz = lax.axis_size("sub")
    above, below = lax.rem(z + 1, nz), lax.rem(z + nz - 1, nz)
    inner = pad.at[:, NJ : NJ + NR]
    pairs = [
        (dest_h, dest), (adj_h, inner), (base_h, base), (frac_h, frac), (cell_h, cell),
        (coef_h, coef), (src_h, src),
    ]
    loads = [pltpu.make_async_copy(a, b, load_sem.at[i]) for i, (a, b) in enumerate(pairs)]
    for load in loads:
        load.start()

    def peer(o):
        return lax.rem(me + o, G)

    barrier = pltpu.get_barrier_semaphore()

    def greet(o, _):
        pl.semaphore_signal(barrier, inc=1, device_id={"blk": peer(o)}, device_id_type=MESH)
        return 0

    lax.fori_loop(1, G, greet, 0)
    for at in (above, below):
        pl.semaphore_signal(barrier, inc=1, device_id={"sub": at}, device_id_type=MESH)

    loads[0].wait()
    find_ranks(dest, rank)
    for load in loads[1:5]:
        load.wait()
    transposed_field(lambda v: pad[v, NJ : NJ + NR], ft, 3)
    interpolate(ft, cell, base, frac, vals, 256, 8)
    pack(vals, dest, rank, pick, send)

    def put(src_ref, dst_ref, o, ssem, rsem):
        to = peer(o)
        return pltpu.make_async_remote_copy(
            src_ref.at[to], dst_ref.at[me], ssem.at[o], rsem.at[me], device_id={"blk": to}, device_id_type=MESH
        )

    def arrived(src_ref, dst_ref, o, ssem, rsem):
        at = peer(o)
        pltpu.make_async_remote_copy(
            src_ref.at[at], dst_ref.at[at], ssem.at[o], rsem.at[at], device_id={"blk": at}, device_id_type=MESH
        ).wait_recv()

    pl.semaphore_wait(barrier, G + 1)

    def start1(o, _):
        put(send, got, o, send1, recv1).start()
        return 0

    def wait1(o, _):
        arrived(send, got, o, send1, recv1)
        return 0

    lax.fori_loop(1, G, start1, 0)
    got[me] = send[me]
    lax.fori_loop(1, G, wait1, 0)

    halos = []
    for first in range(0, NV, VG):
        add_received(got, acc, first, VG, 8)
        for v in range(VG):
            pad[first + v, NJ : NJ + NR] += acc[:, v * NK : (v + 1) * NK]
        part = pad.at[first : first + VG]
        for d, (lo, hi, to) in enumerate(((NR, 0, above), (NJ, NR + NJ, below))):
            slot = first // VG * 2 + d
            halos.append(
                pltpu.make_async_remote_copy(
                    part.at[:, lo : lo + NJ], part.at[:, hi : hi + NJ], halo_send.at[slot], halo_recv.at[slot],
                    device_id={"sub": to}, device_id_type=MESH,
                )
            )
            halos[-1].start()
    for load in loads[5:]:
        load.wait()
    stencil_rows(pad, src, coef, jac, res, NJ, 2 * NJ, 16)
    for halo in halos:
        halo.wait()

    @pl.when(z == 0)
    def _():
        pad[:, 0:NJ] = jnp.zeros((NV, NJ, NK), F32)

    @pl.when(z == nz - 1)
    def _():
        pad[:, NJ + NR :] = jnp.zeros((NV, NJ, NK), F32)

    stencil_rows(pad, src, coef, jac, res, 0, NJ, 16)
    stencil_rows(pad, src, coef, jac, res, NR - NJ, NJ, 16)

    transposed_field(lambda v: res[v], ft, 2)

    def look_up(o, _):
        s = peer(o)
        cell = got[s, 6:7].astype(I32)
        oi = one_hot(cell >> 7, NR)
        ok = rows(NK, CAP) == (cell & 127)
        t = jnp.dot(ft[:, : 2 * NR], jnp.concatenate([oi, oi], axis=0), preferred_element_type=F32)
        line = [
            jnp.sum(jnp.where(ok, t[v * NK : (v + 1) * NK], 0.0), axis=0, keepdims=True)
            for v in range(NV)
        ]
        back[s] = jnp.concatenate(line + [jnp.zeros((2, CAP), F32)], axis=0)
        return 0

    def group(c, _):
        lax.fori_loop(c * 8 + 1, c * 8 + 9, look_up, 0, unroll=True)

        def start2(o, _):
            put(back, ret, o, send2, recv2).start()
            return 0

        lax.fori_loop(c * 8 + 1, jnp.minimum(c * 8 + 9, G), start2, 0)
        return 0

    lax.fori_loop(0, G // 8, group, 0)
    ret[me] = back[me]

    def wait2(o, _):
        arrived(back, ret, o, send2, recv2)
        return 0

    lax.fori_loop(1, G, wait2, 0)
    unpack_and_add(ret, rank, dest, base, frac, parts, sums, 1024, 2)
    for v in range(NV):
        out[v] = res[v] + sums[:, v * NK : (v + 1) * NK]

    def sent(o, _):
        put(send, got, o, send1, recv1).wait_send()
        put(back, ret, o, send2, recv2).wait_send()
        return 0

    lax.fori_loop(1, G, sent, 0)


def per_device(adjoint, source, cell_coef, flux_jacobian, fringe_dest, fringe_cell, fringe_base, fringe_frac):
    any_space = pl.BlockSpec(memory_space=pl.ANY)
    buffer = pltpu.VMEM((G, 8, CAP), F32)
    line = pltpu.VMEM((1, R), I32)
    field = pltpu.VMEM((NV, NR, NK), F32)
    dma = pltpu.SemaphoreType.DMA
    out = pl.pallas_call(
        kernel,
        out_shape=jax.ShapeDtypeStruct((NV, NR, NK), F32),
        in_specs=[any_space] * 7 + [pl.BlockSpec(memory_space=pltpu.SMEM)],
        out_specs=VMEM,
        scratch_shapes=[
            field, pltpu.VMEM((4, NR, NK), F32), line, line, line, pltpu.VMEM((3, R), F32), line,
            pltpu.VMEM((NV * NK, 3 * NR), BF16), pltpu.VMEM((8, R), F32), pltpu.VMEM((G * 16, R), BF16),
            buffer, buffer, buffer, buffer,
            pltpu.VMEM((NV, NR + 2 * NJ, NK), F32), pltpu.VMEM((NR, VG * NK), F32), pltpu.VMEM((NR, NV * NK), F32),
            field, pltpu.VMEM((G * 16, CAP), BF16),
            dma((7,)), dma((G,)), dma((G,)), dma((G,)), dma((G,)), dma((NV // VG * 2,)), dma((NV // VG * 2,)),
        ],
        compiler_params=pltpu.CompilerParams(vmem_limit_bytes=56 << 20, collective_id=0, has_side_effects=True),
        name="adjoint",
    )(
        adjoint.reshape(NV, NR, NK), source.reshape(NV, NR, NK), cell_coef.reshape(4, NR, NK),
        fringe_dest.reshape(1, R), fringe_cell.reshape(1, R), fringe_base.reshape(1, R), fringe_frac,
        flux_jacobian.reshape(3 * 2 * NV * NV),
    )
    return out.reshape(adjoint.shape)


def solution(mesh):
    return jax.shard_map(
        per_device,
        mesh=mesh,
        in_specs=(
            P(None, "blk", "sub", None, None),
            P(None, "blk", "sub", None, None),
            P(None, "blk", "sub", None, None),
            P("blk", None, None, None, None),
            P(("blk", "sub"), None),
            P(("blk", "sub")),
            P(("blk", "sub")),
            P(None, ("blk", "sub")),
        ),
        out_specs=P(None, "blk", "sub", None, None),
        check_vma=False,
    )
```

```python
import functools

import jax
import jax.numpy as jnp
from jax import lax
from jax.experimental import pallas as pl
from jax.experimental.pallas import tpu as pltpu
from jax.sharding import PartitionSpec as P

NV, NI, NJ, NK = 6, 4, 64, 128
NR = NI * NJ
R = 4096
G = 32
CAP = 256
F32, BF16, I32 = jnp.float32, jnp.bfloat16, jnp.int32
VMEM = pl.BlockSpec(memory_space=pltpu.VMEM)
MESH = pl.DeviceIdType.MESH
NT = (((1,), (1,)), ((), ()))


def split(x):
    hi = x.astype(BF16)
    return hi, (x - hi.astype(F32)).astype(BF16)


def rows(n, m):
    return lax.broadcasted_iota(I32, (n, m), 0)


def corner_rows(base, frac, n):
    i0, j0 = base >> 13, (base >> 7) & 63
    f0, f1 = frac[0:1], frac[1:2]
    jj = rows(NJ, n)
    wj = jnp.where(jj == j0, 1.0 - f1, jnp.where(jj == j0 + 1, f1, 0.0))
    parts = []
    for i in range(NI):
        wi = jnp.where(i0 == i, 1.0 - f0, jnp.where(i0 == i - 1, f0, 0.0))
        parts.append(wj * wi)
    return jnp.concatenate(parts, axis=0)


def corner_cols(base, frac, n):
    k0, f2 = base & 127, frac[2:3]
    kk = rows(NK, n)
    return jnp.where(kk == k0, 1.0 - f2, jnp.where(kk == k0 + 1, f2, 0.0))


def transposed_field(field, ft_ref, copies):
    for v in range(NV):
        hi, lo = split(field(v).T)
        at = pl.ds(v * NK, NK)
        for c, part in enumerate((hi, lo, hi)[:copies]):
            ft_ref[at, c * NR : (c + 1) * NR] = part


def one_hot(index, n):
    return (rows(n, index.shape[1]) == index).astype(F32).astype(BF16)


def chunk(c, n):
    return pl.ds(pl.multiple_of(c * n, n), n)


def find_places(dest, place):
    tri = (rows(256, 256) < lax.broadcasted_iota(I32, (256, 256), 1)).astype(F32).astype(BF16)

    def step(c, carry):
        at = chunk(c, 256)
        hot = (rows(G, 256) == dest[:, at]).astype(F32)
        before = jnp.dot(hot.astype(BF16), tri, preferred_element_type=F32) + carry
        place[:, at] = one_hot(jnp.sum(hot * before, axis=0, keepdims=True).astype(I32), CAP)
        return carry + jnp.sum(hot, axis=1, keepdims=True)

    lax.fori_loop(0, R // 256, step, jnp.zeros((G, 1), F32), unroll=True)


def interpolate(ft, cell, base, frac, vals, high, low, cols, n, unroll):
    def step(c, _):
        at = chunk(c, n)
        b, f = base[:, at], frac[:, at]
        hi, lo = split(corner_rows(b, f, n))
        high[:, at], low[:, at] = hi, lo
        t = jnp.dot(ft[...], jnp.concatenate([hi, hi, lo], axis=0), preferred_element_type=F32)
        wk = corner_cols(b, f, n)
        cols[:, at] = wk
        out = [jnp.sum(t[v * NK : (v + 1) * NK] * wk, axis=0, keepdims=True) for v in range(NV)]
        out += [cell[:, at].astype(F32), jnp.zeros((1, n), F32)]
        vals[:, at] = jnp.concatenate(out, axis=0)
        return 0

    lax.fori_loop(0, R // n, step, 0, unroll=unroll)


def pack(vals, dest, place, pick, send):
    hi, lo = split(vals[...])
    both = jnp.concatenate([hi.astype(F32), lo.astype(F32)], axis=0)
    to = jnp.broadcast_to(dest[...], (16, R))

    def step(d, _):
        pick[pl.ds(pl.multiple_of(d * 16, 16), 16)] = jnp.where(to == d, both, 0.0).astype(BF16)
        return 0

    lax.fori_loop(0, G, step, 0, unroll=4)
    t = lax.dot_general(pick[...], place[...], NT, preferred_element_type=F32)
    t = t.reshape(G, 16, CAP)
    send[...] = t[:, :8] + t[:, 8:]


def add_received(got, acc, order, arrive, first, count, u):
    def step(c, _):
        left, right = [], [[] for _ in range(count)]
        for p in range(u):
            if arrive is not None:
                arrive(c * u + p)
            g = got[order(c * u + p)]
            cell = g[6:7].astype(I32)
            oi = one_hot(cell >> 7, NR)
            ok = one_hot(cell & 127, NK)
            hi, lo = split(g)
            left += [oi, oi]
            for v in range(count):
                at = slice(first + v, first + v + 1)
                right[v] += [ok * hi[at], ok * lo[at]]
        left = jnp.concatenate(left, axis=1)
        right = jnp.concatenate([jnp.concatenate(r, axis=1) for r in right], axis=0)
        acc[...] += lax.dot_general(left, right, NT, preferred_element_type=F32)
        return 0

    acc[...] = jnp.zeros_like(acc)
    lax.fori_loop(0, G // u, step, 0)


def stencil_rows(pad, source, coef, jac, res, first, count, tj):
    kk = lax.broadcasted_iota(I32, (tj, NK), 1)

    def step(c, _):
        r0 = pl.multiple_of(first + c * tj, tj)
        jj = (rows(tj, NK) + r0) & (NJ - 1)
        total = [[None] * NV for _ in range(3)]
        mid = [pad[v, pl.ds(r0 + NJ, tj)] for v in range(NV)]

        def add(d, s, v, x):
            for e in range(NV):
                term = jac[d, v, s, e] * x
                total[d][e] = term if total[d][e] is None else total[d][e] + term

        for v in range(NV):
            add(0, 0, v, pad[v, pl.ds(r0 + 2 * NJ, tj)])
            add(0, 1, v, pad[v, pl.ds(r0, tj)])
            add(1, 0, v, jnp.where(jj == NJ - 1, 0.0, pad[v, pl.ds(r0 + NJ + 1, tj)]))
            add(1, 1, v, jnp.where(jj == 0, 0.0, pad[v, pl.ds(r0 + NJ - 1, tj)]))
            add(2, 0, v, jnp.where(kk == NK - 1, 0.0, pltpu.roll(mid[v], NK - 1, 1)))
            add(2, 1, v, jnp.where(kk == 0, 0.0, pltpu.roll(mid[v], 1, 1)))
        at = pl.ds(r0, tj)
        for e in range(NV):
            image = coef[0, at] * mid[e]
            for d in range(3):
                image += coef[d + 1, at] * total[d][e]
            res[e, at] = source[e, at] - image
        return 0

    lax.fori_loop(0, count // tj, step, 0)


def unpack_and_add(ret, place, dest, high, low, cols, parts, acc, n, unroll):
    for d in range(G):
        hi, lo = split(ret[d])
        parts[d * 16 : (d + 1) * 16] = jnp.concatenate([hi.astype(F32), lo.astype(F32)], axis=0).astype(BF16)

    def step(c, _):
        at = chunk(c, n)
        t = jnp.dot(parts[...], place[:, at], preferred_element_type=F32)
        to = jnp.broadcast_to(dest[:, at], (16, n))
        both = jnp.zeros((16, n), F32)
        for d in range(G):
            both = jnp.where(to == d, t[d * 16 : (d + 1) * 16], both)
        value = both[:8] + both[8:]
        ah, al, wk = high[:, at], low[:, at], cols[:, at]
        left = jnp.concatenate([ah, ah, al], axis=1)
        right = []
        for v in range(NV):
            hi, lo = split(wk * value[v : v + 1])
            right.append(jnp.concatenate([hi, lo, hi], axis=1))
        right = jnp.concatenate(right, axis=0)
        acc[...] += lax.dot_general(left, right, NT, preferred_element_type=F32)
        return 0

    acc[...] = jnp.zeros_like(acc)
    lax.fori_loop(0, R // n, step, 0, unroll=unroll)


VG = 2
UP = 8


def kernel(
    adj_h, src_h, coef_h, dest_h, cell_h, base_h, frac_h, jac_h, out,
    src, coef, dest, cell, base, frac, jac, ft, vals, pick, place, high, low, cols,
    send, got, back, ret, pad, rim, acc, sums, res, parts,
    load_sem, send1, recv1, send2, recv2, rim_send, rim_recv,
):
    me, z = lax.axis_index("blk"), lax.axis_index("sub")
    nz = lax.axis_size("sub")
    above, below = lax.rem(z + 1, nz), lax.rem(z + nz - 1, nz)
    inner = pad.at[:, NJ : NJ + NR]
    pairs = [
        (dest_h, dest), (adj_h, inner), (base_h, base), (frac_h, frac), (cell_h, cell),
        (jac_h, jac), (coef_h, coef), (src_h, src),
    ]
    loads = [pltpu.make_async_copy(a, b, load_sem.at[i]) for i, (a, b) in enumerate(pairs)]
    for load in loads:
        load.start()

    def ahead(o):
        return lax.rem(me + o, G)

    def behind(o):
        return lax.rem(me + G - o, G)

    barrier = pltpu.get_barrier_semaphore()

    def greet(o, _):
        pl.semaphore_signal(barrier, inc=1, device_id={"blk": ahead(o)}, device_id_type=MESH)
        return 0

    lax.fori_loop(1, G, greet, 0)
    for at in (above, below):
        pl.semaphore_signal(barrier, inc=1, device_id={"sub": at}, device_id_type=MESH)

    pad[:, 0:NJ] = jnp.zeros((NV, NJ, NK), F32)
    pad[:, NJ + NR :] = jnp.zeros((NV, NJ, NK), F32)
    loads[0].wait()
    find_places(dest, place)
    for load in loads[1:5]:
        load.wait()
    transposed_field(lambda v: pad[v, NJ : NJ + NR], ft, 3)
    interpolate(ft, cell, base, frac, vals, high, low, cols, 256, 8)
    pack(vals, dest, place, pick, send)

    def put(src_ref, dst_ref, n, o, ssem, rsem):
        to = ahead(o)
        return pltpu.make_async_remote_copy(
            src_ref.at[to, 0:n], dst_ref.at[me, 0:n], ssem.at[o], rsem.at[me],
            device_id={"blk": to}, device_id_type=MESH,
        )

    def arrived(src_ref, dst_ref, n, o, ssem, rsem):
        at = behind(o)
        pltpu.make_async_remote_copy(
            src_ref.at[at, 0:n], dst_ref.at[at, 0:n], ssem.at[o], rsem.at[at],
            device_id={"blk": at}, device_id_type=MESH,
        ).wait_recv()

    pl.semaphore_wait(barrier, G + 1)

    def start1(o, _):
        put(send, got, NV + 1, o, send1, recv1).start()
        return 0

    lax.fori_loop(1, G, start1, 0)
    got[me] = send[me]

    def arrive1(o):
        @pl.when(o > 0)
        def _():
            arrived(send, got, NV + 1, o, send1, recv1)

    rims = []
    for first in range(0, NV, VG):
        add_received(got, acc, behind, None if first else arrive1, first, VG, 8)
        for v in range(VG):
            pad[first + v, NJ : NJ + NR] += acc[:, v * NK : (v + 1) * NK]
        part, land = pad.at[first : first + VG], rim.at[:, first : first + VG]
        for d, (row, to) in enumerate(((NR, above), (NJ, below))):
            slot = first // VG * 2 + d
            rims.append(
                pltpu.make_async_remote_copy(
                    part.at[:, row : row + NJ], land.at[d], rim_send.at[slot], rim_recv.at[slot],
                    device_id={"sub": to}, device_id_type=MESH,
                )
            )
            rims[-1].start()
    for load in loads[5:]:
        load.wait()
    stencil_rows(pad, src, coef, jac, res, 0, NR, 16)
    for copy in rims:
        copy.wait()

    def add_rim(d, row):
        def step(c, _):
            at, here = pl.ds(pl.multiple_of(c * 16, 16), 16), pl.ds(pl.multiple_of(row + c * 16, 16), 16)
            for e in range(NV):
                total = jac[0, 0, 1 - d, e] * rim[d, 0, at]
                for v in range(1, NV):
                    total += jac[0, v, 1 - d, e] * rim[d, v, at]
                res[e, here] -= coef[1, here] * total
            return 0

        lax.fori_loop(0, NJ // 16, step, 0)

    @pl.when(z > 0)
    def _():
        add_rim(0, 0)

    @pl.when(z < nz - 1)
    def _():
        add_rim(1, NR - NJ)

    transposed_field(lambda v: res[v], ft, 2)

    def look_up(o):
        s = ahead(o)
        at = got[s, 6:7].astype(I32)
        oi = one_hot(at >> 7, NR)
        ok = rows(NK, CAP) == (at & 127)
        t = jnp.dot(ft[:, : 2 * NR], jnp.concatenate([oi, oi], axis=0), preferred_element_type=F32)
        line = [
            jnp.sum(jnp.where(ok, t[v * NK : (v + 1) * NK], 0.0), axis=0, keepdims=True)
            for v in range(NV)
        ]
        back[s] = jnp.concatenate(line + [jnp.zeros((2, CAP), F32)], axis=0)

    def group(c, _):
        for p in range(UP):
            look_up(c * UP + p + 1)

        def start2(o, _):
            put(back, ret, NV, o, send2, recv2).start()
            return 0

        lax.fori_loop(c * UP + 1, jnp.minimum(c * UP + UP + 1, G), start2, 0)
        return 0

    lax.fori_loop(0, G // UP, group, 0)
    ret[:, NV:] = jnp.zeros((G, 8 - NV, CAP), F32)
    ret[me, 0:NV] = back[me, 0:NV]

    def wait2(o, _):
        arrived(back, ret, NV, o, send2, recv2)
        return 0

    lax.fori_loop(1, G, wait2, 0)
    unpack_and_add(ret, place, dest, high, low, cols, parts, sums, 1024, 2)
    for v in range(NV):
        out[v] = res[v] + sums[:, v * NK : (v + 1) * NK]

    def sent(o, _):
        put(send, got, NV + 1, o, send1, recv1).wait_send()
        put(back, ret, NV, o, send2, recv2).wait_send()
        return 0

    lax.fori_loop(1, G, sent, 0)


def per_device(adjoint, source, cell_coef, flux_jacobian, fringe_dest, fringe_cell, fringe_base, fringe_frac):
    any_space = pl.BlockSpec(memory_space=pl.ANY)
    buffer = pltpu.VMEM((G, 8, CAP), F32)
    line = pltpu.VMEM((1, R), I32)
    field = pltpu.VMEM((NV, NR, NK), F32)
    dma = pltpu.SemaphoreType.DMA
    copies = NV // VG * 2
    arrays = (
        adjoint.reshape(NV, NR, NK), source.reshape(NV, NR, NK), cell_coef.reshape(4, NR, NK),
        fringe_dest.reshape(1, R), fringe_cell.reshape(1, R), fringe_base.reshape(1, R), fringe_frac,
        flux_jacobian[0].transpose(0, 2, 1, 3),
    )
    arrays = [pltpu.with_memory_space_constraint(x, pltpu.HBM) for x in arrays]
    out = pl.pallas_call(
        kernel,
        out_shape=jax.ShapeDtypeStruct((NV, NR, NK), F32),
        in_specs=[any_space] * 8,
        out_specs=VMEM,
        scratch_shapes=[
            field, pltpu.VMEM((4, NR, NK), F32), line, line, line, pltpu.VMEM((3, R), F32),
            pltpu.SMEM((3, NV, 2, NV), F32),
            pltpu.VMEM((NV * NK, 3 * NR), BF16), pltpu.VMEM((8, R), F32), pltpu.VMEM((G * 16, R), BF16),
            pltpu.VMEM((CAP, R), BF16), pltpu.VMEM((NR, R), BF16), pltpu.VMEM((NR, R), BF16), pltpu.VMEM((NK, R), F32),
            buffer, buffer, buffer, buffer,
            pltpu.VMEM((NV, NR + 2 * NJ, NK), F32), pltpu.VMEM((2, NV, NJ, NK), F32),
            pltpu.VMEM((NR, VG * NK), F32), pltpu.VMEM((NR, NV * NK), F32),
            field, pltpu.VMEM((G * 16, CAP), BF16),
            dma((8,)), dma((G,)), dma((G,)), dma((G,)), dma((G,)), dma((copies,)), dma((copies,)),
        ],
        compiler_params=pltpu.CompilerParams(vmem_limit_bytes=48 << 20, collective_id=0, has_side_effects=True),
        name="adjoint",
    )(*arrays)
    return out.reshape(adjoint.shape)


def solution(mesh):
    return jax.shard_map(
        per_device,
        mesh=mesh,
        in_specs=(
            P(None, "blk", "sub", None, None),
            P(None, "blk", "sub", None, None),
            P(None, "blk", "sub", None, None),
            P("blk", None, None, None, None),
            P(("blk", "sub"), None),
            P(("blk", "sub")),
            P(("blk", "sub")),
            P(None, ("blk", "sub")),
        ),
        out_specs=P(None, "blk", "sub", None, None),
        check_vma=False,
    )
```

```python
import functools

import jax
import jax.numpy as jnp
from jax import lax
from jax.experimental import pallas as pl
from jax.experimental.pallas import tpu as pltpu
from jax.sharding import PartitionSpec as P

NV, NI, NJ, NK = 6, 4, 64, 128
NR = NI * NJ
R = 4096
G = 32
CAP = 256
F32, BF16, I32 = jnp.float32, jnp.bfloat16, jnp.int32
VMEM = pl.BlockSpec(memory_space=pltpu.VMEM)
MESH = pl.DeviceIdType.MESH
NT = (((1,), (1,)), ((), ()))


def split(x):
    hi = x.astype(BF16)
    return hi, (x - hi.astype(F32)).astype(BF16)


def rows(n, m):
    return lax.broadcasted_iota(I32, (n, m), 0)


def corner_rows(base, frac, n):
    i0, j0 = base >> 13, (base >> 7) & 63
    f0, f1 = frac[0:1], frac[1:2]
    jj = rows(NJ, n)
    wj = jnp.where(jj == j0, 1.0 - f1, jnp.where(jj == j0 + 1, f1, 0.0))
    parts = []
    for i in range(NI):
        wi = jnp.where(i0 == i, 1.0 - f0, jnp.where(i0 == i - 1, f0, 0.0))
        parts.append(wj * wi)
    return jnp.concatenate(parts, axis=0)


def corner_cols(base, frac, n):
    k0, f2 = base & 127, frac[2:3]
    kk = rows(NK, n)
    return jnp.where(kk == k0, 1.0 - f2, jnp.where(kk == k0 + 1, f2, 0.0))


def transposed_field(field, ft_ref, copies):
    for v in range(NV):
        hi, lo = split(field(v).T)
        at = pl.ds(v * NK, NK)
        for c, part in enumerate((hi, lo, hi)[:copies]):
            ft_ref[at, c * NR : (c + 1) * NR] = part


def one_hot(index, n):
    m = index.shape[1]
    hit = rows(n, m).astype(F32).astype(BF16) == index.astype(F32).astype(BF16)
    return jnp.where(hit, jnp.ones((n, m), BF16), jnp.zeros((n, m), BF16))


def chunk(c, n):
    return pl.ds(pl.multiple_of(c * n, n), n)


def find_places(dest, place):
    tri = (rows(256, 256) < lax.broadcasted_iota(I32, (256, 256), 1)).astype(F32).astype(BF16)

    def step(c, carry):
        at = chunk(c, 256)
        hot = (rows(G, 256) == dest[:, at]).astype(F32)
        before = jnp.dot(hot.astype(BF16), tri, preferred_element_type=F32) + carry
        place[:, at] = one_hot(jnp.sum(hot * before, axis=0, keepdims=True).astype(I32), CAP)
        return carry + jnp.sum(hot, axis=1, keepdims=True)

    lax.fori_loop(0, R // 256, step, jnp.zeros((G, 1), F32), unroll=True)


def interpolate(ft, cell, base, frac, vals, high, low, cols, n, unroll):
    def step(c, _):
        at = chunk(c, n)
        b, f = base[:, at], frac[:, at]
        hi, lo = split(corner_rows(b, f, n))
        high[:, at], low[:, at] = hi, lo
        t = jnp.dot(ft[...], jnp.concatenate([hi, hi, lo], axis=0), preferred_element_type=F32)
        wk = corner_cols(b, f, n)
        cols[:, at] = wk
        out = [jnp.sum(t[v * NK : (v + 1) * NK] * wk, axis=0, keepdims=True) for v in range(NV)]
        out += [cell[:, at].astype(F32), jnp.zeros((1, n), F32)]
        vals[:, at] = jnp.concatenate(out, axis=0)
        return 0

    lax.fori_loop(0, R // n, step, 0, unroll=unroll)


def pack(vals, offset, place, pick, send, launch):
    both = jnp.concatenate(split(vals[...]), axis=0)
    to = jnp.broadcast_to(offset.astype(F32).astype(BF16), (16, R))
    for o in range(G):
        pick[o * 16 : (o + 1) * 16] = jnp.where(to == jnp.bfloat16(o), both, jnp.zeros_like(both))
    part = G // 2
    for first in (0, part):
        t = lax.dot_general(pick[first * 16 : (first + part) * 16], place[...], NT, preferred_element_type=F32)
        t = t.reshape(part, 16, CAP)
        send[first : first + part] = t[:, :8] + t[:, 8:]
        for o in range(first, first + part):
            launch(o)


def add_received(got, acc, order, arrive, first, count, u):
    def step(c, _):
        left, right = [], [[] for _ in range(count)]
        if arrive is not None:
            for p in range(u):
                arrive(c * u + p + 1, p == u - 1)
        for p in range(u):
            g = got[order(c * u + p + 1)]
            cell = g[6:7].astype(I32)
            oi = one_hot(cell >> 7, NR)
            ok = one_hot(cell & 127, NK)
            hi, lo = split(g)
            left += [oi, oi]
            for v in range(count):
                at = slice(first + v, first + v + 1)
                right[v] += [ok * hi[at], ok * lo[at]]
        left = jnp.concatenate(left, axis=1)
        right = jnp.concatenate([jnp.concatenate(r, axis=1) for r in right], axis=0)
        acc[...] += lax.dot_general(left, right, NT, preferred_element_type=F32)
        return 0

    acc[...] = jnp.zeros_like(acc)
    lax.fori_loop(0, G // u, step, 0)


def stencil_rows(pad, source, coef, jac, res, first, count, tj):
    kk = lax.broadcasted_iota(I32, (tj, NK), 1)

    def step(c, _):
        r0 = pl.multiple_of(first + c * tj, tj)
        jj = (rows(tj, NK) + r0) & (NJ - 1)
        total = [[None] * NV for _ in range(3)]
        mid = [pad[v, pl.ds(r0 + NJ, tj)] for v in range(NV)]

        def add(d, s, v, x):
            for e in range(NV):
                term = jac[d, v, s, e] * x
                total[d][e] = term if total[d][e] is None else total[d][e] + term

        for v in range(NV):
            add(0, 0, v, pad[v, pl.ds(r0 + 2 * NJ, tj)])
            add(0, 1, v, pad[v, pl.ds(r0, tj)])
            add(1, 0, v, jnp.where(jj == NJ - 1, 0.0, pad[v, pl.ds(r0 + NJ + 1, tj)]))
            add(1, 1, v, jnp.where(jj == 0, 0.0, pad[v, pl.ds(r0 + NJ - 1, tj)]))
            add(2, 0, v, jnp.where(kk == NK - 1, 0.0, pltpu.roll(mid[v], NK - 1, 1)))
            add(2, 1, v, jnp.where(kk == 0, 0.0, pltpu.roll(mid[v], 1, 1)))
        at = pl.ds(r0, tj)
        for e in range(NV):
            image = coef[0, at] * mid[e]
            for d in range(3):
                image += coef[d + 1, at] * total[d][e]
            res[e, at] = source[e, at] - image
        return 0

    lax.fori_loop(0, count // tj, step, 0)


def unpack_and_add(ret, place, dest, high, low, cols, parts, acc, n, unroll):
    for d in range(G):
        hi, lo = split(ret[d])
        parts[d * 16 : (d + 1) * 16] = jnp.concatenate([hi.astype(F32), lo.astype(F32)], axis=0).astype(BF16)

    def step(c, _):
        at = chunk(c, n)
        t = jnp.dot(parts[...], place[:, at], preferred_element_type=F32)
        to = jnp.broadcast_to(dest[:, at], (16, n))
        both = jnp.zeros((16, n), F32)
        for d in range(G):
            both = jnp.where(to == d, t[d * 16 : (d + 1) * 16], both)
        value = both[:8] + both[8:]
        ah, al, wk = high[:, at], low[:, at], cols[:, at]
        left = jnp.concatenate([ah, ah, al], axis=1)
        right = []
        for v in range(NV):
            hi, lo = split(wk * value[v : v + 1])
            right.append(jnp.concatenate([hi, lo, hi], axis=1))
        right = jnp.concatenate(right, axis=0)
        acc[...] += lax.dot_general(left, right, NT, preferred_element_type=F32)
        return 0

    acc[...] = jnp.zeros_like(acc)
    lax.fori_loop(0, R // n, step, 0, unroll=unroll)


VG = 2
UP = 8


def kernel(
    adj_h, src_h, coef_h, dest_h, cell_h, base_h, frac_h, jac_h, out,
    src, coef, dest, cell, base, frac, jac, ft, vals, pick, place, high, low, cols,
    send, got, back, ret, pad, rim, acc, sums, res, parts,
    load_sem, send1, recv1, send2, recv2, rim_send, rim_recv,
):
    me, z = lax.axis_index("blk"), lax.axis_index("sub")
    nz = lax.axis_size("sub")
    above, below = lax.rem(z + 1, nz), lax.rem(z + nz - 1, nz)
    inner = pad.at[:, NJ : NJ + NR]
    pairs = [
        (dest_h, dest), (adj_h, inner), (base_h, base), (frac_h, frac), (cell_h, cell),
        (jac_h, jac), (coef_h, coef), (src_h, src),
    ]
    loads = [pltpu.make_async_copy(a, b, load_sem.at[i]) for i, (a, b) in enumerate(pairs)]
    for load in loads:
        load.start()

    def ahead(o):
        return lax.rem(me + o, G)

    def behind(o):
        return lax.rem(me + G - o, G)

    barrier = pltpu.get_barrier_semaphore()

    def greet(o, _):
        pl.semaphore_signal(barrier, inc=1, device_id={"blk": ahead(o)}, device_id_type=MESH)
        return 0

    lax.fori_loop(1, G, greet, 0, unroll=True)
    for at in (above, below):
        pl.semaphore_signal(barrier, inc=1, device_id={"sub": at}, device_id_type=MESH)

    pad[:, 0:NJ] = jnp.zeros((NV, NJ, NK), F32)
    pad[:, NJ + NR :] = jnp.zeros((NV, NJ, NK), F32)
    loads[0].wait()
    find_places(dest, place)
    for load in loads[1:5]:
        load.wait()
    transposed_field(lambda v: pad[v, NJ : NJ + NR], ft, 3)
    interpolate(ft, cell, base, frac, vals, high, low, cols, 256, 16)
    pl.semaphore_wait(barrier, G + 1)

    def put(src, dst_ref, n, o, ssem, rsem):
        return pltpu.make_async_remote_copy(
            src.at[0:n], dst_ref.at[me, 0:n], ssem.at[o], rsem.at[me],
            device_id={"blk": ahead(o)}, device_id_type=MESH,
        )

    def arrived(dst_ref, n, o, ssem, rsem):
        at = behind(o)
        pltpu.make_async_remote_copy(
            dst_ref.at[at, 0:n], dst_ref.at[at, 0:n], ssem.at[o], rsem.at[at],
            device_id={"blk": at}, device_id_type=MESH,
        ).wait_recv()

    def put1(o):
        return put(send.at[o], got, NV + 1, o, send1, recv1)

    def put2(o):
        return put(back.at[ahead(o)], ret, NV, o, send2, recv2)

    def launch(o):
        if o:
            put1(o).start()

    pack(vals, (dest[...] - me) & (G - 1), place, pick, send, launch)
    got[me] = send[0]

    def arrive1(o, may_be_own):
        if may_be_own:
            pl.when(o < G)(lambda: arrived(got, NV + 1, o, send1, recv1))
        else:
            arrived(got, NV + 1, o, send1, recv1)

    rims = []
    for first in range(0, NV, VG):
        add_received(got, acc, behind, None if first else arrive1, first, VG, 16 if first else 8)
        for v in range(VG):
            pad[first + v, NJ : NJ + NR] += acc[:, v * NK : (v + 1) * NK]
        part, land = pad.at[first : first + VG], rim.at[:, first : first + VG]
        for d, (row, to) in enumerate(((NR, above), (NJ, below))):
            slot = first // VG * 2 + d
            rims.append(
                pltpu.make_async_remote_copy(
                    part.at[:, row : row + NJ], land.at[d], rim_send.at[slot], rim_recv.at[slot],
                    device_id={"sub": to}, device_id_type=MESH,
                )
            )
            rims[-1].start()
    for load in loads[5:]:
        load.wait()
    stencil_rows(pad, src, coef, jac, res, 0, NR, 16)
    for copy in rims:
        copy.wait()

    def add_rim(d, row):
        def step(c, _):
            at, here = pl.ds(pl.multiple_of(c * 16, 16), 16), pl.ds(pl.multiple_of(row + c * 16, 16), 16)
            for e in range(NV):
                total = jac[0, 0, 1 - d, e] * rim[d, 0, at]
                for v in range(1, NV):
                    total += jac[0, v, 1 - d, e] * rim[d, v, at]
                res[e, here] -= coef[1, here] * total
            return 0

        lax.fori_loop(0, NJ // 16, step, 0)

    @pl.when(z > 0)
    def _():
        add_rim(0, 0)

    @pl.when(z < nz - 1)
    def _():
        add_rim(1, NR - NJ)

    transposed_field(lambda v: res[v], ft, 2)

    def look_up(o):
        s = ahead(o)
        at = got[s, 6:7].astype(I32)
        oi = one_hot(at >> 7, NR)
        ok = rows(NK, CAP) == (at & 127)
        t = jnp.dot(ft[:, : 2 * NR], jnp.concatenate([oi, oi], axis=0), preferred_element_type=F32)
        line = [
            jnp.sum(jnp.where(ok, t[v * NK : (v + 1) * NK], 0.0), axis=0, keepdims=True)
            for v in range(NV)
        ]
        back[s] = jnp.concatenate(line + [jnp.zeros((2, CAP), F32)], axis=0)

    ready = []
    for o in list(range(1, G)):
        if o % UP == 1:
            while ready:
                put2(ready.pop(0)).start()
        look_up(o)
        ready.append(o)
    while ready:
        put2(ready.pop(0)).start()
    look_up(0)

    def sent(o, _):
        put1(o).wait_send()
        put2(o).wait_send()
        return 0

    lax.fori_loop(1, G, sent, 0)
    ret[:, NV:] = jnp.zeros((G, 8 - NV, CAP), F32)
    ret[me, 0:NV] = back[me, 0:NV]

    def wait2(o, _):
        arrived(ret, NV, o, send2, recv2)
        return 0

    lax.fori_loop(1, G, wait2, 0)
    unpack_and_add(ret, place, dest, high, low, cols, parts, sums, 1024, 2)
    for v in range(NV):
        out[v] = res[v] + sums[:, v * NK : (v + 1) * NK]


def per_device(adjoint, source, cell_coef, flux_jacobian, fringe_dest, fringe_cell, fringe_base, fringe_frac):
    any_space = pl.BlockSpec(memory_space=pl.ANY)
    buffer = pltpu.VMEM((G, 8, CAP), F32)
    line = pltpu.VMEM((1, R), I32)
    field = pltpu.VMEM((NV, NR, NK), F32)
    dma = pltpu.SemaphoreType.DMA
    copies = NV // VG * 2
    arrays = (
        adjoint.reshape(NV, NR, NK), source.reshape(NV, NR, NK), cell_coef.reshape(4, NR, NK),
        fringe_dest.reshape(1, R), fringe_cell.reshape(1, R), fringe_base.reshape(1, R), fringe_frac,
        flux_jacobian[0].transpose(0, 2, 1, 3),
    )
    arrays = [pltpu.with_memory_space_constraint(x, pltpu.HBM) for x in arrays]
    out = pl.pallas_call(
        kernel,
        out_shape=jax.ShapeDtypeStruct((NV, NR, NK), F32),
        in_specs=[any_space] * 8,
        out_specs=VMEM,
        scratch_shapes=[
            field, pltpu.VMEM((4, NR, NK), F32), line, line, line, pltpu.VMEM((3, R), F32),
            pltpu.SMEM((3, NV, 2, NV), F32),
            pltpu.VMEM((NV * NK, 3 * NR), BF16), pltpu.VMEM((8, R), F32), pltpu.VMEM((G * 16, R), BF16),
            pltpu.VMEM((CAP, R), BF16), pltpu.VMEM((NR, R), BF16), pltpu.VMEM((NR, R), BF16), pltpu.VMEM((NK, R), F32),
            buffer, buffer, buffer, buffer,
            pltpu.VMEM((NV, NR + 2 * NJ, NK), F32), pltpu.VMEM((2, NV, NJ, NK), F32),
            pltpu.VMEM((NR, VG * NK), F32), pltpu.VMEM((NR, NV * NK), F32),
            field, pltpu.VMEM((G * 16, CAP), BF16),
            dma((8,)), dma((G,)), dma((G,)), dma((G,)), dma((G,)), dma((copies,)), dma((copies,)),
        ],
        compiler_params=pltpu.CompilerParams(vmem_limit_bytes=48 << 20, collective_id=0, has_side_effects=True),
        name="adjoint",
    )(*arrays)
    return out.reshape(adjoint.shape)


def solution(mesh):
    return jax.shard_map(
        per_device,
        mesh=mesh,
        in_specs=(
            P(None, "blk", "sub", None, None),
            P(None, "blk", "sub", None, None),
            P(None, "blk", "sub", None, None),
            P("blk", None, None, None, None),
            P(("blk", "sub"), None),
            P(("blk", "sub")),
            P(("blk", "sub")),
            P(None, ("blk", "sub")),
        ),
        out_specs=P(None, "blk", "sub", None, None),
        check_vma=False,
    )
```

```python
import functools

import jax
import jax.numpy as jnp
from jax import lax
from jax.experimental import pallas as pl
from jax.experimental.pallas import tpu as pltpu
from jax.sharding import PartitionSpec as P

NV, NI, NJ, NK = 6, 4, 64, 128
NR = NI * NJ
R = 4096
G = 32
CAP = 256
F32, BF16, I32 = jnp.float32, jnp.bfloat16, jnp.int32
VMEM = pl.BlockSpec(memory_space=pltpu.VMEM)
MESH = pl.DeviceIdType.MESH
NT = (((1,), (1,)), ((), ()))


def split(x):
    hi = x.astype(BF16)
    return hi, (x - hi.astype(F32)).astype(BF16)


def rows(n, m):
    return lax.broadcasted_iota(I32, (n, m), 0)


def corner_rows(base, frac, n):
    i0, j0 = base >> 13, (base >> 7) & 63
    f0, f1 = frac[0:1], frac[1:2]
    jj = rows(NJ, n)
    wj = jnp.where(jj == j0, 1.0 - f1, jnp.where(jj == j0 + 1, f1, 0.0))
    parts = []
    for i in range(NI):
        wi = jnp.where(i0 == i, 1.0 - f0, jnp.where(i0 == i - 1, f0, 0.0))
        parts.append(wj * wi)
    return jnp.concatenate(parts, axis=0)


def corner_cols(base, frac, n):
    k0, f2 = base & 127, frac[2:3]
    kk = rows(NK, n)
    return jnp.where(kk == k0, 1.0 - f2, jnp.where(kk == k0 + 1, f2, 0.0))


def transposed_field(field, ft_ref, copies):
    for v in range(NV):
        hi, lo = split(field(v).T)
        at = pl.ds(v * NK, NK)
        for c, part in enumerate((hi, lo, hi)[:copies]):
            ft_ref[at, c * NR : (c + 1) * NR] = part


def one_hot(index, n):
    m = index.shape[1]
    hit = rows(n, m).astype(F32).astype(BF16) == index.astype(F32).astype(BF16)
    return jnp.where(hit, jnp.ones((n, m), BF16), jnp.zeros((n, m), BF16))


def chunk(c, n):
    return pl.ds(pl.multiple_of(c * n, n), n)


def find_places(dest, place):
    tri = (rows(256, 256) < lax.broadcasted_iota(I32, (256, 256), 1)).astype(F32).astype(BF16)

    def step(c, carry):
        at = chunk(c, 256)
        hot = (rows(G, 256) == dest[:, at]).astype(F32)
        before = jnp.dot(hot.astype(BF16), tri, preferred_element_type=F32) + carry
        place[:, at] = one_hot(jnp.sum(hot * before, axis=0, keepdims=True).astype(I32), CAP)
        return carry + jnp.sum(hot, axis=1, keepdims=True)

    lax.fori_loop(0, R // 256, step, jnp.zeros((G, 1), F32), unroll=True)


def interpolate(ft, cell, base, frac, vals, high, low, cols, n, unroll):
    def step(c, _):
        at = chunk(c, n)
        b, f = base[:, at], frac[:, at]
        hi, lo = split(corner_rows(b, f, n))
        high[:, at], low[:, at] = hi, lo
        t = jnp.dot(ft[...], jnp.concatenate([hi, hi, lo], axis=0), preferred_element_type=F32)
        wk = corner_cols(b, f, n)
        cols[:, at] = wk
        out = [jnp.sum(t[v * NK : (v + 1) * NK] * wk, axis=0, keepdims=True) for v in range(NV)]
        out += [cell[:, at].astype(F32), jnp.zeros((1, n), F32)]
        vals[:, at] = jnp.concatenate(out, axis=0)
        return 0

    lax.fori_loop(0, R // n, step, 0, unroll=unroll)


def pack(vals, offset, place, pick, send, launch):
    both = jnp.concatenate(split(vals[...]), axis=0)
    to = jnp.broadcast_to(offset.astype(F32).astype(BF16), (16, R))
    for o in range(G):
        pick[o * 16 : (o + 1) * 16] = jnp.where(to == jnp.bfloat16(o), both, jnp.zeros_like(both))
    part = G // 2
    for first in (0, part):
        t = lax.dot_general(pick[first * 16 : (first + part) * 16], place[...], NT, preferred_element_type=F32)
        t = t.reshape(part, 16, CAP)
        send[first : first + part] = t[:, :8] + t[:, 8:]
        for o in range(first, first + part):
            launch(o)


def add_received(got, acc, order, arrive, first, count, u):
    def step(c, _):
        left, right = [], [[] for _ in range(count)]
        if arrive is not None:
            for p in range(u):
                arrive(c * u + p + 1, p == u - 1)
        for p in range(u):
            g = got[order(c * u + p + 1)]
            cell = g[6:7].astype(I32)
            oi = one_hot(cell >> 7, NR)
            ok = one_hot(cell & 127, NK)
            hi, lo = split(g)
            left += [oi, oi]
            for v in range(count):
                at = slice(first + v, first + v + 1)
                right[v] += [ok * hi[at], ok * lo[at]]
        left = jnp.concatenate(left, axis=1)
        right = jnp.concatenate([jnp.concatenate(r, axis=1) for r in right], axis=0)
        acc[...] += lax.dot_general(left, right, NT, preferred_element_type=F32)
        return 0

    acc[...] = jnp.zeros_like(acc)
    lax.fori_loop(0, G // u, step, 0)


def stencil_rows(pad, source, coef, jac, res, first, count, tj):
    kk = lax.broadcasted_iota(I32, (tj, NK), 1)

    def step(c, _):
        r0 = pl.multiple_of(first + c * tj, tj)
        jj = (rows(tj, NK) + r0) & (NJ - 1)
        total = [[None] * NV for _ in range(3)]
        mid = [pad[v, pl.ds(r0 + NJ, tj)] for v in range(NV)]

        def add(d, s, v, x):
            for e in range(NV):
                term = jac[d, v, s, e] * x
                total[d][e] = term if total[d][e] is None else total[d][e] + term

        for v in range(NV):
            add(0, 0, v, pad[v, pl.ds(r0 + 2 * NJ, tj)])
            add(0, 1, v, pad[v, pl.ds(r0, tj)])
            add(1, 0, v, jnp.where(jj == NJ - 1, 0.0, pad[v, pl.ds(r0 + NJ + 1, tj)]))
            add(1, 1, v, jnp.where(jj == 0, 0.0, pad[v, pl.ds(r0 + NJ - 1, tj)]))
            add(2, 0, v, jnp.where(kk == NK - 1, 0.0, pltpu.roll(mid[v], NK - 1, 1)))
            add(2, 1, v, jnp.where(kk == 0, 0.0, pltpu.roll(mid[v], 1, 1)))
        at = pl.ds(r0, tj)
        for e in range(NV):
            image = coef[0, at] * mid[e]
            for d in range(3):
                image += coef[d + 1, at] * total[d][e]
            res[e, at] = source[e, at] - image
        return 0

    lax.fori_loop(0, count // tj, step, 0)


def unpack_and_add(ret, place, dest, high, low, cols, parts, vals, acc, n, unroll):
    for d in range(G):
        hi, lo = split(ret[d])
        parts[d * 16 : (d + 1) * 16] = jnp.concatenate([hi.astype(F32), lo.astype(F32)], axis=0).astype(BF16)

    def step(c, _):
        at = chunk(c, n)
        t = jnp.dot(parts[...], place[:, at], preferred_element_type=F32)
        to = jnp.broadcast_to(dest[:, at], (16, n))
        both = jnp.zeros((16, n), F32)
        for d in range(G):
            both = jnp.where(to == d, t[d * 16 : (d + 1) * 16], both)
        vals[:, at] = both[:8] + both[8:]
        return 0

    lax.fori_loop(0, R // n, step, 0, unroll=unroll)

    def step(c, _):
        at = chunk(c, n)
        value = vals[:, at]
        ah, al, wk = high[:, at], low[:, at], cols[:, at]
        left = jnp.concatenate([ah, ah, al], axis=1)
        right = []
        for v in range(NV):
            hi, lo = split(wk * value[v : v + 1])
            right.append(jnp.concatenate([hi, lo, hi], axis=1))
        right = jnp.concatenate(right, axis=0)
        acc[...] += lax.dot_general(left, right, NT, preferred_element_type=F32)
        return 0

    acc[...] = jnp.zeros_like(acc)
    lax.fori_loop(0, R // n, step, 0, unroll=unroll)


VG = 2
UP = 8


def kernel(
    adj_h, src_h, coef_h, dest_h, cell_h, base_h, frac_h, jac_h, out,
    src, coef, dest, cell, base, frac, jac, ft, vals, pick, place, high, low, cols,
    send, got, back, ret, pad, rim, acc, sums, res, parts,
    load_sem, send1, recv1, send2, recv2, rim_send, rim_recv,
):
    me, z = lax.axis_index("blk"), lax.axis_index("sub")
    nz = lax.axis_size("sub")
    above, below = lax.rem(z + 1, nz), lax.rem(z + nz - 1, nz)
    inner = pad.at[:, NJ : NJ + NR]
    pairs = [
        (dest_h, dest), (adj_h, inner), (base_h, base), (frac_h, frac), (cell_h, cell),
        (jac_h, jac), (coef_h, coef), (src_h, src),
    ]
    loads = [pltpu.make_async_copy(a, b, load_sem.at[i]) for i, (a, b) in enumerate(pairs)]
    for load in loads:
        load.start()

    def ahead(o):
        return lax.rem(me + o, G)

    def behind(o):
        return lax.rem(me + G - o, G)

    barrier = pltpu.get_barrier_semaphore()

    def greet(o, _):
        pl.semaphore_signal(barrier, inc=1, device_id={"blk": ahead(o)}, device_id_type=MESH)
        return 0

    lax.fori_loop(1, G, greet, 0, unroll=True)
    for at in (above, below):
        pl.semaphore_signal(barrier, inc=1, device_id={"sub": at}, device_id_type=MESH)

    pad[:, 0:NJ] = jnp.zeros((NV, NJ, NK), F32)
    pad[:, NJ + NR :] = jnp.zeros((NV, NJ, NK), F32)
    loads[0].wait()
    find_places(dest, place)
    for load in loads[1:5]:
        load.wait()
    transposed_field(lambda v: pad[v, NJ : NJ + NR], ft, 3)
    interpolate(ft, cell, base, frac, vals, high, low, cols, 256, 16)
    pl.semaphore_wait(barrier, G + 1)

    def put(src, dst_ref, n, o, ssem, rsem):
        return pltpu.make_async_remote_copy(
            src.at[0:n], dst_ref.at[me, 0:n], ssem.at[o], rsem.at[me],
            device_id={"blk": ahead(o)}, device_id_type=MESH,
        )

    def arrived(dst_ref, n, o, ssem, rsem):
        at = behind(o)
        pltpu.make_async_remote_copy(
            dst_ref.at[at, 0:n], dst_ref.at[at, 0:n], ssem.at[o], rsem.at[at],
            device_id={"blk": at}, device_id_type=MESH,
        ).wait_recv()

    def put1(o):
        return put(send.at[o], got, NV + 1, o, send1, recv1)

    def put2(o):
        return put(back.at[ahead(o)], ret, NV, o, send2, recv2)

    def launch(o):
        if o:
            put1(o).start()

    pack(vals, (dest[...] - me) & (G - 1), place, pick, send, launch)
    got[me] = send[0]

    def arrive1(o, may_be_own):
        if may_be_own:
            pl.when(o < G)(lambda: arrived(got, NV + 1, o, send1, recv1))
        else:
            arrived(got, NV + 1, o, send1, recv1)

    rims = []
    for first in range(0, NV, VG):
        add_received(got, acc, behind, None if first else arrive1, first, VG, 32 if first else 8)
        for v in range(VG):
            pad[first + v, NJ : NJ + NR] += acc[:, v * NK : (v + 1) * NK]
        part, land = pad.at[first : first + VG], rim.at[:, first : first + VG]
        for d, (row, to) in enumerate(((NR, above), (NJ, below))):
            slot = first // VG * 2 + d
            rims.append(
                pltpu.make_async_remote_copy(
                    part.at[:, row : row + NJ], land.at[d], rim_send.at[slot], rim_recv.at[slot],
                    device_id={"sub": to}, device_id_type=MESH,
                )
            )
            rims[-1].start()
    for load in loads[5:]:
        load.wait()
    stencil_rows(pad, src, coef, jac, res, 0, NR, 16)
    for copy in rims:
        copy.wait()

    def add_rim(d, row):
        def step(c, _):
            at, here = pl.ds(pl.multiple_of(c * 16, 16), 16), pl.ds(pl.multiple_of(row + c * 16, 16), 16)
            for e in range(NV):
                total = jac[0, 0, 1 - d, e] * rim[d, 0, at]
                for v in range(1, NV):
                    total += jac[0, v, 1 - d, e] * rim[d, v, at]
                res[e, here] -= coef[1, here] * total
            return 0

        lax.fori_loop(0, NJ // 16, step, 0)

    @pl.when(z > 0)
    def _():
        add_rim(0, 0)

    @pl.when(z < nz - 1)
    def _():
        add_rim(1, NR - NJ)

    transposed_field(lambda v: res[v], ft, 2)

    def look_up(o):
        s = ahead(o)
        at = got[s, 6:7].astype(I32)
        oi = one_hot(at >> 7, NR)
        ok = rows(NK, CAP) == (at & 127)
        t = jnp.dot(ft[:, : 2 * NR], jnp.concatenate([oi, oi], axis=0), preferred_element_type=F32)
        line = [
            jnp.sum(jnp.where(ok, t[v * NK : (v + 1) * NK], 0.0), axis=0, keepdims=True)
            for v in range(NV)
        ]
        back[s] = jnp.concatenate(line + [jnp.zeros((2, CAP), F32)], axis=0)

    ready = []
    for o in list(range(1, G)):
        if o % UP == 1:
            while ready:
                put2(ready.pop(0)).start()
        look_up(o)
        ready.append(o)
    while ready:
        put2(ready.pop(0)).start()
    look_up(0)

    def sent(o, _):
        put1(o).wait_send()
        put2(o).wait_send()
        return 0

    lax.fori_loop(1, G, sent, 0)
    ret[:, NV:] = jnp.zeros((G, 8 - NV, CAP), F32)
    ret[me, 0:NV] = back[me, 0:NV]

    def wait2(o, _):
        arrived(ret, NV, o, send2, recv2)
        return 0

    lax.fori_loop(1, G, wait2, 0)
    unpack_and_add(ret, place, dest, high, low, cols, parts, vals, sums, 1024, 2)
    for v in range(NV):
        out[v] = res[v] + sums[:, v * NK : (v + 1) * NK]


def per_device(adjoint, source, cell_coef, flux_jacobian, fringe_dest, fringe_cell, fringe_base, fringe_frac):
    any_space = pl.BlockSpec(memory_space=pl.ANY)
    buffer = pltpu.VMEM((G, 8, CAP), F32)
    line = pltpu.VMEM((1, R), I32)
    field = pltpu.VMEM((NV, NR, NK), F32)
    dma = pltpu.SemaphoreType.DMA
    copies = NV // VG * 2
    arrays = (
        adjoint.reshape(NV, NR, NK), source.reshape(NV, NR, NK), cell_coef.reshape(4, NR, NK),
        fringe_dest.reshape(1, R), fringe_cell.reshape(1, R), fringe_base.reshape(1, R), fringe_frac,
        flux_jacobian[0].transpose(0, 2, 1, 3),
    )
    arrays = [pltpu.with_memory_space_constraint(x, pltpu.HBM) for x in arrays]
    out = pl.pallas_call(
        kernel,
        out_shape=jax.ShapeDtypeStruct((NV, NR, NK), F32),
        in_specs=[any_space] * 8,
        out_specs=VMEM,
        scratch_shapes=[
            field, pltpu.VMEM((4, NR, NK), F32), line, line, line, pltpu.VMEM((3, R), F32),
            pltpu.SMEM((3, NV, 2, NV), F32),
            pltpu.VMEM((NV * NK, 3 * NR), BF16), pltpu.VMEM((8, R), F32), pltpu.VMEM((G * 16, R), BF16),
            pltpu.VMEM((CAP, R), BF16), pltpu.VMEM((NR, R), BF16), pltpu.VMEM((NR, R), BF16), pltpu.VMEM((NK, R), F32),
            buffer, buffer, buffer, buffer,
            pltpu.VMEM((NV, NR + 2 * NJ, NK), F32), pltpu.VMEM((2, NV, NJ, NK), F32),
            pltpu.VMEM((NR, VG * NK), F32), pltpu.VMEM((NR, NV * NK), F32),
            field, pltpu.VMEM((G * 16, CAP), BF16),
            dma((8,)), dma((G,)), dma((G,)), dma((G,)), dma((G,)), dma((copies,)), dma((copies,)),
        ],
        compiler_params=pltpu.CompilerParams(vmem_limit_bytes=48 << 20, collective_id=0, has_side_effects=True),
        name="adjoint",
    )(*arrays)
    return out.reshape(adjoint.shape)


def solution(mesh):
    return jax.shard_map(
        per_device,
        mesh=mesh,
        in_specs=(
            P(None, "blk", "sub", None, None),
            P(None, "blk", "sub", None, None),
            P(None, "blk", "sub", None, None),
            P("blk", None, None, None, None),
            P(("blk", "sub"), None),
            P(("blk", "sub")),
            P(("blk", "sub")),
            P(None, ("blk", "sub")),
        ),
        out_specs=P(None, "blk", "sub", None, None),
        check_vma=False,
    )
```

```python
import functools

import jax
import jax.numpy as jnp
from jax import lax
from jax.experimental import pallas as pl
from jax.experimental.pallas import tpu as pltpu
from jax.sharding import PartitionSpec as P

NV, NI, NJ, NK = 6, 4, 64, 128
NR = NI * NJ
R = 4096
G = 32
CAP = 256
F32, BF16, I32 = jnp.float32, jnp.bfloat16, jnp.int32
VMEM = pl.BlockSpec(memory_space=pltpu.VMEM)
MESH = pl.DeviceIdType.MESH
NT = (((1,), (1,)), ((), ()))


def split(x):
    hi = x.astype(BF16)
    return hi, (x - hi.astype(F32)).astype(BF16)


def rows(n, m):
    return lax.broadcasted_iota(I32, (n, m), 0)


def corner_rows(base, frac, n):
    i0, j0 = base >> 13, (base >> 7) & 63
    f0, f1 = frac[0:1], frac[1:2]
    jj = rows(NJ, n)
    wj = jnp.where(jj == j0, 1.0 - f1, jnp.where(jj == j0 + 1, f1, 0.0))
    parts = []
    for i in range(NI):
        wi = jnp.where(i0 == i, 1.0 - f0, jnp.where(i0 == i - 1, f0, 0.0))
        parts.append(wj * wi)
    return jnp.concatenate(parts, axis=0)


def corner_cols(base, frac, n):
    k0, f2 = base & 127, frac[2:3]
    kk = rows(NK, n)
    return jnp.where(kk == k0, 1.0 - f2, jnp.where(kk == k0 + 1, f2, 0.0))


def transposed_field(field, ft_ref, copies):
    for v in range(NV):
        hi, lo = split(field(v).T)
        at = pl.ds(v * NK, NK)
        for c, part in enumerate((hi, lo, hi)[:copies]):
            ft_ref[at, c * NR : (c + 1) * NR] = part


def one_hot(index, n):
    m = index.shape[1]
    hit = rows(n, m).astype(F32).astype(BF16) == index.astype(F32).astype(BF16)
    return jnp.where(hit, jnp.ones((n, m), BF16), jnp.zeros((n, m), BF16))


def chunk(c, n):
    return pl.ds(pl.multiple_of(c * n, n), n)


def find_places(dest, place):
    tri = (rows(256, 256) < lax.broadcasted_iota(I32, (256, 256), 1)).astype(F32).astype(BF16)

    def step(c, carry):
        at = chunk(c, 256)
        hot = (rows(G, 256) == dest[:, at]).astype(F32)
        before = jnp.dot(hot.astype(BF16), tri, preferred_element_type=F32) + carry
        place[:, at] = one_hot(jnp.sum(hot * before, axis=0, keepdims=True).astype(I32), CAP)
        return carry + jnp.sum(hot, axis=1, keepdims=True)

    lax.fori_loop(0, R // 256, step, jnp.zeros((G, 1), F32), unroll=True)


def interpolate(ft, cell, base, frac, vals, high, low, cols, n, unroll):
    def step(c, _):
        at = chunk(c, n)
        b, f = base[:, at], frac[:, at]
        hi, lo = split(corner_rows(b, f, n))
        high[:, at], low[:, at] = hi, lo
        t = jnp.dot(ft[...], jnp.concatenate([hi, hi, lo], axis=0), preferred_element_type=F32)
        wk = corner_cols(b, f, n)
        cols[:, at] = wk
        out = [jnp.sum(t[v * NK : (v + 1) * NK] * wk, axis=0, keepdims=True) for v in range(NV)]
        out += [cell[:, at].astype(F32), jnp.zeros((1, n), F32)]
        vals[:, at] = jnp.concatenate(out, axis=0)
        return 0

    lax.fori_loop(0, R // n, step, 0, unroll=unroll)


def pack(vals, offset, place, pick, send, launch):
    both = jnp.concatenate(split(vals[...]), axis=0)
    to = jnp.broadcast_to(offset.astype(F32).astype(BF16), (16, R))
    for o in range(G):
        pick[o * 16 : (o + 1) * 16] = jnp.where(to == jnp.bfloat16(o), both, jnp.zeros_like(both))
    part = G // 2
    for first in (0, part):
        t = lax.dot_general(pick[first * 16 : (first + part) * 16], place[...], NT, preferred_element_type=F32)
        t = t.reshape(part, 16, CAP)
        send[first : first + part] = t[:, :8] + t[:, 8:]
        for o in range(first, first + part):
            launch(o)


def add_received(got, acc, order, arrive, first, count, u):
    def step(c, _):
        left, right = [], [[] for _ in range(count)]
        if arrive is not None:
            for p in range(u):
                arrive(c * u + p + 1, p == u - 1)
        for p in range(u):
            g = got[order(c * u + p + 1)]
            cell = g[6:7].astype(I32)
            oi = one_hot(cell >> 7, NR)
            ok = one_hot(cell & 127, NK)
            hi, lo = split(g)
            left += [oi, oi]
            for v in range(count):
                at = slice(first + v, first + v + 1)
                right[v] += [ok * hi[at], ok * lo[at]]
        left = jnp.concatenate(left, axis=1)
        right = jnp.concatenate([jnp.concatenate(r, axis=1) for r in right], axis=0)
        acc[...] += lax.dot_general(left, right, NT, preferred_element_type=F32)
        return 0

    acc[...] = jnp.zeros_like(acc)
    lax.fori_loop(0, G // u, step, 0)


def stencil_rows(pad, source, coef, jac, res, first, count, tj):
    kk = lax.broadcasted_iota(I32, (tj, NK), 1)

    def step(c, _):
        r0 = pl.multiple_of(first + c * tj, tj)
        jj = (rows(tj, NK) + r0) & (NJ - 1)
        total = [[None] * NV for _ in range(3)]
        mid = [pad[v, pl.ds(r0 + NJ, tj)] for v in range(NV)]

        def add(d, s, v, x):
            for e in range(NV):
                term = jac[d, v, s, e] * x
                total[d][e] = term if total[d][e] is None else total[d][e] + term

        for v in range(NV):
            add(0, 0, v, pad[v, pl.ds(r0 + 2 * NJ, tj)])
            add(0, 1, v, pad[v, pl.ds(r0, tj)])
            add(1, 0, v, jnp.where(jj == NJ - 1, 0.0, pad[v, pl.ds(r0 + NJ + 1, tj)]))
            add(1, 1, v, jnp.where(jj == 0, 0.0, pad[v, pl.ds(r0 + NJ - 1, tj)]))
            add(2, 0, v, jnp.where(kk == NK - 1, 0.0, pltpu.roll(mid[v], NK - 1, 1)))
            add(2, 1, v, jnp.where(kk == 0, 0.0, pltpu.roll(mid[v], 1, 1)))
        at = pl.ds(r0, tj)
        for e in range(NV):
            image = coef[0, at] * mid[e]
            for d in range(3):
                image += coef[d + 1, at] * total[d][e]
            res[e, at] = source[e, at] - image
        return 0

    lax.fori_loop(0, count // tj, step, 0)


def unpack_and_add(ret, place, dest, high, low, cols, parts, vals, acc, n, unroll):
    for d in range(G):
        hi, lo = split(ret[d])
        parts[d * 16 : (d + 1) * 16] = jnp.concatenate([hi.astype(F32), lo.astype(F32)], axis=0).astype(BF16)

    def step(c, _):
        at = chunk(c, n)
        t = jnp.dot(parts[...], place[:, at], preferred_element_type=F32)
        to = jnp.broadcast_to(dest[:, at], (16, n))
        both = jnp.zeros((16, n), F32)
        for d in range(G):
            both = jnp.where(to == d, t[d * 16 : (d + 1) * 16], both)
        vals[:, at] = both[:8] + both[8:]
        return 0

    lax.fori_loop(0, R // n, step, 0, unroll=unroll)

    def step(c, _):
        at = chunk(c, n)
        value = vals[:, at]
        ah, al, wk = high[:, at], low[:, at], cols[:, at]
        left = jnp.concatenate([ah, ah, al], axis=1)
        right = []
        for v in range(NV):
            hi, lo = split(wk * value[v : v + 1])
            right.append(jnp.concatenate([hi, lo, hi], axis=1))
        right = jnp.concatenate(right, axis=0)
        acc[...] += lax.dot_general(left, right, NT, preferred_element_type=F32)
        return 0

    acc[...] = jnp.zeros_like(acc)
    lax.fori_loop(0, R // n, step, 0, unroll=unroll)


VG = 2
UP = 8


def kernel(
    adj_h, src_h, coef_h, dest_h, cell_h, base_h, frac_h, jac_h, out,
    src, coef, dest, cell, base, frac, jac, ft, vals, pick, place, high, low, cols,
    send, got, back, ret, pad, rim, acc, sums, res, parts,
    load_sem, send1, recv1, send2, recv2, rim_send, rim_recv,
):
    me, z = lax.axis_index("blk"), lax.axis_index("sub")
    nz = lax.axis_size("sub")
    above, below = lax.rem(z + 1, nz), lax.rem(z + nz - 1, nz)
    inner = pad.at[:, NJ : NJ + NR]
    pairs = [
        (dest_h, dest), (adj_h, inner), (base_h, base), (frac_h, frac), (cell_h, cell),
        (jac_h, jac), (coef_h, coef), (src_h, src),
    ]
    loads = [pltpu.make_async_copy(a, b, load_sem.at[i]) for i, (a, b) in enumerate(pairs)]
    for load in loads:
        load.start()

    def ahead(o):
        return lax.rem(me + o, G)

    def behind(o):
        return lax.rem(me + G - o, G)

    barrier = pltpu.get_barrier_semaphore()

    def greet(o, _):
        pl.semaphore_signal(barrier, inc=1, device_id={"blk": ahead(o)}, device_id_type=MESH)
        return 0

    lax.fori_loop(1, G, greet, 0, unroll=True)
    for at in (above, below):
        pl.semaphore_signal(barrier, inc=1, device_id={"sub": at}, device_id_type=MESH)

    pad[:, 0:NJ] = jnp.zeros((NV, NJ, NK), F32)
    pad[:, NJ + NR :] = jnp.zeros((NV, NJ, NK), F32)
    loads[0].wait()
    find_places(dest, place)
    for load in loads[1:5]:
        load.wait()
    transposed_field(lambda v: pad[v, NJ : NJ + NR], ft, 3)
    interpolate(ft, cell, base, frac, vals, high, low, cols, 256, 16)
    pl.semaphore_wait(barrier, G + 1)

    def put(src, dst_ref, n, o, ssem, rsem):
        return pltpu.make_async_remote_copy(
            src.at[0:n], dst_ref.at[me, 0:n], ssem.at[o], rsem.at[me],
            device_id={"blk": ahead(o)}, device_id_type=MESH,
        )

    def arrived(dst_ref, n, o, ssem, rsem):
        at = behind(o)
        pltpu.make_async_remote_copy(
            dst_ref.at[at, 0:n], dst_ref.at[at, 0:n], ssem.at[o], rsem.at[at],
            device_id={"blk": at}, device_id_type=MESH,
        ).wait_recv()

    def put1(o):
        return put(send.at[o], got, NV + 1, o, send1, recv1)

    def put2(o):
        return put(back.at[ahead(o)], ret, NV, o, send2, recv2)

    def launch(o):
        if o:
            put1(o).start()

    pack(vals, (dest[...] - me) & (G - 1), place, pick, send, launch)
    got[me] = send[0]

    def arrive1(o, may_be_own):
        if may_be_own:
            pl.when(o < G)(lambda: arrived(got, NV + 1, o, send1, recv1))
        else:
            arrived(got, NV + 1, o, send1, recv1)

    rims = []
    for first in range(0, NV, VG):
        add_received(got, acc, behind, None if first else arrive1, first, VG, 16 if first else 8)
        for v in range(VG):
            pad[first + v, NJ : NJ + NR] += acc[:, v * NK : (v + 1) * NK]
        part, land = pad.at[first : first + VG], rim.at[:, first : first + VG]
        for d, (row, to) in enumerate(((NR, above), (NJ, below))):
            slot = first // VG * 2 + d
            rims.append(
                pltpu.make_async_remote_copy(
                    part.at[:, row : row + NJ], land.at[d], rim_send.at[slot], rim_recv.at[slot],
                    device_id={"sub": to}, device_id_type=MESH,
                )
            )
            rims[-1].start()
    for load in loads[5:]:
        load.wait()
    stencil_rows(pad, src, coef, jac, res, 0, NR, 16)
    for copy in rims:
        copy.wait()

    def add_rim(d, row):
        def step(c, _):
            at, here = pl.ds(pl.multiple_of(c * 16, 16), 16), pl.ds(pl.multiple_of(row + c * 16, 16), 16)
            for e in range(NV):
                total = jac[0, 0, 1 - d, e] * rim[d, 0, at]
                for v in range(1, NV):
                    total += jac[0, v, 1 - d, e] * rim[d, v, at]
                res[e, here] -= coef[1, here] * total
            return 0

        lax.fori_loop(0, NJ // 16, step, 0)

    @pl.when(z > 0)
    def _():
        add_rim(0, 0)

    @pl.when(z < nz - 1)
    def _():
        add_rim(1, NR - NJ)

    transposed_field(lambda v: res[v], ft, 2)

    def look_up(o):
        s = ahead(o)
        at = got[s, 6:7].astype(I32)
        oi = one_hot(at >> 7, NR)
        ok = rows(NK, CAP) == (at & 127)
        t = jnp.dot(ft[:, : 2 * NR], jnp.concatenate([oi, oi], axis=0), preferred_element_type=F32)
        line = [
            jnp.sum(jnp.where(ok, t[v * NK : (v + 1) * NK], 0.0), axis=0, keepdims=True)
            for v in range(NV)
        ]
        back[s] = jnp.concatenate(line + [jnp.zeros((2, CAP), F32)], axis=0)

    ready = []
    for o in list(range(1, G)):
        if o % UP == 1:
            while ready:
                put2(ready.pop(0)).start()
        look_up(o)
        ready.append(o)
    while ready:
        put2(ready.pop(0)).start()
    look_up(0)

    def sent(o, _):
        put1(o).wait_send()
        put2(o).wait_send()
        return 0

    lax.fori_loop(1, G, sent, 0)
    ret[:, NV:] = jnp.zeros((G, 8 - NV, CAP), F32)
    ret[me, 0:NV] = back[me, 0:NV]

    def wait2(o, _):
        arrived(ret, NV, o, send2, recv2)
        return 0

    lax.fori_loop(1, G, wait2, 0)
    unpack_and_add(ret, place, dest, high, low, cols, parts, vals, sums, 1024, 2)
    for v in range(NV):
        out[v] = res[v] + sums[:, v * NK : (v + 1) * NK]


def per_device(adjoint, source, cell_coef, flux_jacobian, fringe_dest, fringe_cell, fringe_base, fringe_frac):
    any_space = pl.BlockSpec(memory_space=pl.ANY)
    buffer = pltpu.VMEM((G, 8, CAP), F32)
    line = pltpu.VMEM((1, R), I32)
    field = pltpu.VMEM((NV, NR, NK), F32)
    dma = pltpu.SemaphoreType.DMA
    copies = NV // VG * 2
    arrays = (
        adjoint.reshape(NV, NR, NK), source.reshape(NV, NR, NK), cell_coef.reshape(4, NR, NK),
        fringe_dest.reshape(1, R), fringe_cell.reshape(1, R), fringe_base.reshape(1, R), fringe_frac,
        flux_jacobian[0].transpose(0, 2, 1, 3),
    )
    arrays = [pltpu.with_memory_space_constraint(x, pltpu.HBM) for x in arrays]
    out = pl.pallas_call(
        kernel,
        out_shape=jax.ShapeDtypeStruct((NV, NR, NK), F32),
        in_specs=[any_space] * 8,
        out_specs=VMEM,
        scratch_shapes=[
            field, pltpu.VMEM((4, NR, NK), F32), line, line, line, pltpu.VMEM((3, R), F32),
            pltpu.SMEM((3, NV, 2, NV), F32),
            pltpu.VMEM((NV * NK, 3 * NR), BF16), pltpu.VMEM((8, R), F32), pltpu.VMEM((G * 16, R), BF16),
            pltpu.VMEM((CAP, R), BF16), pltpu.VMEM((NR, R), BF16), pltpu.VMEM((NR, R), BF16), pltpu.VMEM((NK, R), F32),
            buffer, buffer, buffer, buffer,
            pltpu.VMEM((NV, NR + 2 * NJ, NK), F32), pltpu.VMEM((2, NV, NJ, NK), F32),
            pltpu.VMEM((NR, VG * NK), F32), pltpu.VMEM((NR, NV * NK), F32),
            field, pltpu.VMEM((G * 16, CAP), BF16),
            dma((8,)), dma((G,)), dma((G,)), dma((G,)), dma((G,)), dma((copies,)), dma((copies,)),
        ],
        compiler_params=pltpu.CompilerParams(vmem_limit_bytes=48 << 20, collective_id=0, has_side_effects=True),
        name="adjoint",
    )(*arrays)
    return out.reshape(adjoint.shape)


def solution(mesh):
    return jax.shard_map(
        per_device,
        mesh=mesh,
        in_specs=(
            P(None, "blk", "sub", None, None),
            P(None, "blk", "sub", None, None),
            P(None, "blk", "sub", None, None),
            P("blk", None, None, None, None),
            P(("blk", "sub"), None),
            P(("blk", "sub")),
            P(("blk", "sub")),
            P(None, ("blk", "sub")),
        ),
        out_specs=P(None, "blk", "sub", None, None),
        check_vma=False,
    )
```

```python
import functools

import jax
import jax.numpy as jnp
from jax import lax
from jax.experimental import pallas as pl
from jax.experimental.pallas import tpu as pltpu
from jax.sharding import PartitionSpec as P

NV, NI, NJ, NK = 6, 4, 64, 128
NR = NI * NJ
R = 4096
G = 32
CAP = 256
F32, BF16, I32 = jnp.float32, jnp.bfloat16, jnp.int32
VMEM = pl.BlockSpec(memory_space=pltpu.VMEM)
MESH = pl.DeviceIdType.MESH
NT = (((1,), (1,)), ((), ()))


def split(x):
    hi = x.astype(BF16)
    return hi, (x - hi.astype(F32)).astype(BF16)


def rows(n, m):
    return lax.broadcasted_iota(I32, (n, m), 0)


def corner_rows(base, frac, n):
    i0, j0 = base >> 13, (base >> 7) & 63
    f0, f1 = frac[0:1], frac[1:2]
    jj = rows(NJ, n)
    wj = jnp.where(jj == j0, 1.0 - f1, jnp.where(jj == j0 + 1, f1, 0.0))
    parts = []
    for i in range(NI):
        wi = jnp.where(i0 == i, 1.0 - f0, jnp.where(i0 == i - 1, f0, 0.0))
        parts.append(wj * wi)
    return jnp.concatenate(parts, axis=0)


def corner_cols(base, frac, n):
    k0, f2 = base & 127, frac[2:3]
    kk = rows(NK, n)
    return jnp.where(kk == k0, 1.0 - f2, jnp.where(kk == k0 + 1, f2, 0.0))


def transposed_field(field, ft_ref, copies):
    for v in range(NV):
        hi, lo = split(field(v).T)
        at = pl.ds(v * NK, NK)
        for c, part in enumerate((hi, lo, hi)[:copies]):
            ft_ref[at, c * NR : (c + 1) * NR] = part


def one_hot(index, n):
    m = index.shape[1]
    hit = rows(n, m).astype(F32).astype(BF16) == index.astype(F32).astype(BF16)
    return jnp.where(hit, jnp.ones((n, m), BF16), jnp.zeros((n, m), BF16))


def chunk(c, n):
    return pl.ds(pl.multiple_of(c * n, n), n)


def find_places(dest, place):
    tri = (rows(256, 256) < lax.broadcasted_iota(I32, (256, 256), 1)).astype(F32).astype(BF16)

    def step(c, carry):
        at = chunk(c, 256)
        hot = (rows(G, 256) == dest[:, at]).astype(F32)
        before = jnp.dot(hot.astype(BF16), tri, preferred_element_type=F32) + carry
        place[:, at] = one_hot(jnp.sum(hot * before, axis=0, keepdims=True).astype(I32), CAP)
        return carry + jnp.sum(hot, axis=1, keepdims=True)

    lax.fori_loop(0, R // 256, step, jnp.zeros((G, 1), F32), unroll=True)


def interpolate(ft, cell, base, frac, vals, high, low, cols, n, unroll):
    def step(c, _):
        at = chunk(c, n)
        b, f = base[:, at], frac[:, at]
        hi, lo = split(corner_rows(b, f, n))
        high[:, at], low[:, at] = hi, lo
        t = jnp.dot(ft[...], jnp.concatenate([hi, hi, lo], axis=0), preferred_element_type=F32)
        wk = corner_cols(b, f, n)
        cols[:, at] = wk
        out = [jnp.sum(t[v * NK : (v + 1) * NK] * wk, axis=0, keepdims=True) for v in range(NV)]
        out += [cell[:, at].astype(F32), jnp.zeros((1, n), F32)]
        vals[:, at] = jnp.concatenate(out, axis=0)
        return 0

    lax.fori_loop(0, R // n, step, 0, unroll=unroll)


def pack(vals, offset, place, pick, send, launch):
    both = jnp.concatenate(split(vals[...]), axis=0)
    to = jnp.broadcast_to(offset.astype(F32).astype(BF16), (16, R))
    for o in range(G):
        pick[o * 16 : (o + 1) * 16] = jnp.where(to == jnp.bfloat16(o), both, jnp.zeros_like(both))
    part = G // 2
    for first in (0, part):
        t = lax.dot_general(pick[first * 16 : (first + part) * 16], place[...], NT, preferred_element_type=F32)
        t = t.reshape(part, 16, CAP)
        send[first : first + part] = t[:, :8] + t[:, 8:]
        for o in range(first, first + part):
            launch(o)


def add_received(got, acc, order, arrive, first, count, u):
    def step(c, _):
        left, right = [], [[] for _ in range(count)]
        if arrive is not None:
            for p in range(u):
                arrive(c * u + p + 1, p == u - 1)
        for p in range(u):
            g = got[order(c * u + p + 1)]
            cell = g[6:7].astype(I32)
            oi = one_hot(cell >> 7, NR)
            ok = one_hot(cell & 127, NK)
            hi, lo = split(g)
            left += [oi, oi]
            for v in range(count):
                at = slice(first + v, first + v + 1)
                right[v] += [ok * hi[at], ok * lo[at]]
        left = jnp.concatenate(left, axis=1)
        right = jnp.concatenate([jnp.concatenate(r, axis=1) for r in right], axis=0)
        acc[...] += lax.dot_general(left, right, NT, preferred_element_type=F32)
        return 0

    acc[...] = jnp.zeros_like(acc)
    lax.fori_loop(0, G // u, step, 0)


def stencil_rows(pad, source, coef, jac, res, first, count, tj):
    kk = lax.broadcasted_iota(I32, (tj, NK), 1)

    def step(c, _):
        r0 = pl.multiple_of(first + c * tj, tj)
        jj = (rows(tj, NK) + r0) & (NJ - 1)
        total = [[None] * NV for _ in range(3)]
        mid = [pad[v, pl.ds(r0 + NJ, tj)] for v in range(NV)]

        def add(d, s, v, x):
            for e in range(NV):
                term = jac[d, v, s, e] * x
                total[d][e] = term if total[d][e] is None else total[d][e] + term

        for v in range(NV):
            add(0, 0, v, pad[v, pl.ds(r0 + 2 * NJ, tj)])
            add(0, 1, v, pad[v, pl.ds(r0, tj)])
            add(1, 0, v, jnp.where(jj == NJ - 1, 0.0, pad[v, pl.ds(r0 + NJ + 1, tj)]))
            add(1, 1, v, jnp.where(jj == 0, 0.0, pad[v, pl.ds(r0 + NJ - 1, tj)]))
            add(2, 0, v, jnp.where(kk == NK - 1, 0.0, pltpu.roll(mid[v], NK - 1, 1)))
            add(2, 1, v, jnp.where(kk == 0, 0.0, pltpu.roll(mid[v], 1, 1)))
        at = pl.ds(r0, tj)
        for e in range(NV):
            image = coef[0, at] * mid[e]
            for d in range(3):
                image += coef[d + 1, at] * total[d][e]
            res[e, at] = source[e, at] - image
        return 0

    lax.fori_loop(0, count // tj, step, 0)


def unpack_and_add(ret, place, dest, high, low, cols, parts, vals, acc, n, unroll):
    for d in range(G):
        hi, lo = split(ret[d])
        parts[d * 16 : (d + 1) * 16] = jnp.concatenate([hi.astype(F32), lo.astype(F32)], axis=0).astype(BF16)

    def step(c, _):
        at = chunk(c, n)
        t = jnp.dot(parts[...], place[:, at], preferred_element_type=F32)
        to = jnp.broadcast_to(dest[:, at], (16, n))
        both = jnp.zeros((16, n), F32)
        for d in range(G):
            both = jnp.where(to == d, t[d * 16 : (d + 1) * 16], both)
        vals[:, at] = both[:8] + both[8:]
        return 0

    lax.fori_loop(0, R // n, step, 0, unroll=unroll)

    def step(c, _):
        at = chunk(c, n)
        value = vals[:, at]
        ah, al, wk = high[:, at], low[:, at], cols[:, at]
        left = jnp.concatenate([ah, ah, al], axis=1)
        right = []
        for v in range(NV):
            hi, lo = split(wk * value[v : v + 1])
            right.append(jnp.concatenate([hi, lo, hi], axis=1))
        right = jnp.concatenate(right, axis=0)
        acc[...] += lax.dot_general(left, right, NT, preferred_element_type=F32)
        return 0

    acc[...] = jnp.zeros_like(acc)
    lax.fori_loop(0, R // n, step, 0, unroll=unroll)


VG = 2
UP = 8


def kernel(
    adj_h, src_h, coef_h, dest_h, cell_h, base_h, frac_h, jac_h, out,
    src, coef, dest, cell, base, frac, jac, ft, vals, pick, place, high, low, cols,
    send, got, back, ret, pad, rim, acc, sums, res, parts,
    load_sem, send1, recv1, send2, recv2, rim_send, rim_recv,
):
    me, z = lax.axis_index("blk"), lax.axis_index("sub")
    nz = lax.axis_size("sub")
    above, below = lax.rem(z + 1, nz), lax.rem(z + nz - 1, nz)
    inner = pad.at[:, NJ : NJ + NR]
    pairs = [
        (dest_h, dest), (adj_h, inner), (base_h, base), (frac_h, frac), (cell_h, cell),
        (jac_h, jac), (coef_h, coef), (src_h, src),
    ]
    loads = [pltpu.make_async_copy(a, b, load_sem.at[i]) for i, (a, b) in enumerate(pairs)]
    for load in loads:
        load.start()

    def ahead(o):
        return lax.rem(me + o, G)

    def behind(o):
        return lax.rem(me + G - o, G)

    barrier = pltpu.get_barrier_semaphore()

    def greet(o, _):
        pl.semaphore_signal(barrier, inc=1, device_id={"blk": ahead(o)}, device_id_type=MESH)
        return 0

    lax.fori_loop(1, G, greet, 0, unroll=True)
    for at in (above, below):
        pl.semaphore_signal(barrier, inc=1, device_id={"sub": at}, device_id_type=MESH)

    pad[:, 0:NJ] = jnp.zeros((NV, NJ, NK), F32)
    pad[:, NJ + NR :] = jnp.zeros((NV, NJ, NK), F32)
    loads[0].wait()
    find_places(dest, place)
    for load in loads[1:5]:
        load.wait()
    transposed_field(lambda v: pad[v, NJ : NJ + NR], ft, 3)
    interpolate(ft, cell, base, frac, vals, high, low, cols, 256, 16)
    pl.semaphore_wait(barrier, G + 1)

    def put(src, dst_ref, n, o, ssem, rsem):
        return pltpu.make_async_remote_copy(
            src.at[0:n], dst_ref.at[me, 0:n], ssem.at[o], rsem.at[me],
            device_id={"blk": ahead(o)}, device_id_type=MESH,
        )

    def arrived(dst_ref, n, o, ssem, rsem):
        at = behind(o)
        pltpu.make_async_remote_copy(
            dst_ref.at[at, 0:n], dst_ref.at[at, 0:n], ssem.at[o], rsem.at[at],
            device_id={"blk": at}, device_id_type=MESH,
        ).wait_recv()

    def put1(o):
        return put(send.at[o], got, NV + 1, o, send1, recv1)

    def put2(o):
        return put(back.at[ahead(o)], ret, NV, o, send2, recv2)

    def launch(o):
        if o:
            put1(o).start()

    pack(vals, (dest[...] - me) & (G - 1), place, pick, send, launch)
    got[me] = send[0]

    def arrive1(o, may_be_own):
        if may_be_own:
            pl.when(o < G)(lambda: arrived(got, NV + 1, o, send1, recv1))
        else:
            arrived(got, NV + 1, o, send1, recv1)

    rims = []
    for first in range(0, NV, VG):
        add_received(got, acc, behind, None if first else arrive1, first, VG, 16 if first else 8)
        for v in range(VG):
            pad[first + v, NJ : NJ + NR] += acc[:, v * NK : (v + 1) * NK]
        part, land = pad.at[first : first + VG], rim.at[:, first : first + VG]
        for d, (row, to) in enumerate(((NR, above), (NJ, below))):
            slot = first // VG * 2 + d
            rims.append(
                pltpu.make_async_remote_copy(
                    part.at[:, row : row + NJ], land.at[d], rim_send.at[slot], rim_recv.at[slot],
                    device_id={"sub": to}, device_id_type=MESH,
                )
            )
            rims[-1].start()
    for load in loads[5:]:
        load.wait()
    stencil_rows(pad, src, coef, jac, res, 0, NR, 16)
    for copy in rims:
        copy.wait()

    def add_rim(d, row):
        def step(c, _):
            at, here = pl.ds(pl.multiple_of(c * 16, 16), 16), pl.ds(pl.multiple_of(row + c * 16, 16), 16)
            for e in range(NV):
                total = jac[0, 0, 1 - d, e] * rim[d, 0, at]
                for v in range(1, NV):
                    total += jac[0, v, 1 - d, e] * rim[d, v, at]
                res[e, here] -= coef[1, here] * total
            return 0

        lax.fori_loop(0, NJ // 16, step, 0)

    @pl.when(z > 0)
    def _():
        add_rim(0, 0)

    @pl.when(z < nz - 1)
    def _():
        add_rim(1, NR - NJ)

    transposed_field(lambda v: res[v], ft, 2)

    def look_up(o):
        s = ahead(o)
        at = got[s, 6:7].astype(I32)
        oi = one_hot(at >> 7, NR)
        ok = rows(NK, CAP) == (at & 127)
        t = jnp.dot(ft[:, : 2 * NR], jnp.concatenate([oi, oi], axis=0), preferred_element_type=F32)
        line = [
            jnp.sum(jnp.where(ok, t[v * NK : (v + 1) * NK], 0.0), axis=0, keepdims=True)
            for v in range(NV)
        ]
        back[s] = jnp.concatenate(line + [jnp.zeros((2, CAP), F32)], axis=0)

    def start2(o, _):
        put2(o).start()
        return 0

    for first in range(1, G, UP):
        last = min(first + UP, G)
        for o in range(first, last):
            look_up(o)
        lax.fori_loop(first, last, start2, 0)
    look_up(0)

    def sent(o, _):
        put1(o).wait_send()
        put2(o).wait_send()
        return 0

    lax.fori_loop(1, G, sent, 0)
    ret[:, NV:] = jnp.zeros((G, 8 - NV, CAP), F32)
    ret[me, 0:NV] = back[me, 0:NV]

    def wait2(o, _):
        arrived(ret, NV, o, send2, recv2)
        return 0

    lax.fori_loop(1, G, wait2, 0)
    unpack_and_add(ret, place, dest, high, low, cols, parts, vals, sums, 1024, 2)
    for v in range(NV):
        out[v] = res[v] + sums[:, v * NK : (v + 1) * NK]


def per_device(adjoint, source, cell_coef, flux_jacobian, fringe_dest, fringe_cell, fringe_base, fringe_frac):
    any_space = pl.BlockSpec(memory_space=pl.ANY)
    buffer = pltpu.VMEM((G, 8, CAP), F32)
    line = pltpu.VMEM((1, R), I32)
    field = pltpu.VMEM((NV, NR, NK), F32)
    dma = pltpu.SemaphoreType.DMA
    copies = NV // VG * 2
    arrays = (
        adjoint.reshape(NV, NR, NK), source.reshape(NV, NR, NK), cell_coef.reshape(4, NR, NK),
        fringe_dest.reshape(1, R), fringe_cell.reshape(1, R), fringe_base.reshape(1, R), fringe_frac,
        flux_jacobian[0].transpose(0, 2, 1, 3),
    )
    arrays = [pltpu.with_memory_space_constraint(x, pltpu.HBM) for x in arrays]
    out = pl.pallas_call(
        kernel,
        out_shape=jax.ShapeDtypeStruct((NV, NR, NK), F32),
        in_specs=[any_space] * 8,
        out_specs=VMEM,
        scratch_shapes=[
            field, pltpu.VMEM((4, NR, NK), F32), line, line, line, pltpu.VMEM((3, R), F32),
            pltpu.SMEM((3, NV, 2, NV), F32),
            pltpu.VMEM((NV * NK, 3 * NR), BF16), pltpu.VMEM((8, R), F32), pltpu.VMEM((G * 16, R), BF16),
            pltpu.VMEM((CAP, R), BF16), pltpu.VMEM((NR, R), BF16), pltpu.VMEM((NR, R), BF16), pltpu.VMEM((NK, R), F32),
            buffer, buffer, buffer, buffer,
            pltpu.VMEM((NV, NR + 2 * NJ, NK), F32), pltpu.VMEM((2, NV, NJ, NK), F32),
            pltpu.VMEM((NR, VG * NK), F32), pltpu.VMEM((NR, NV * NK), F32),
            field, pltpu.VMEM((G * 16, CAP), BF16),
            dma((8,)), dma((G,)), dma((G,)), dma((G,)), dma((G,)), dma((copies,)), dma((copies,)),
        ],
        compiler_params=pltpu.CompilerParams(vmem_limit_bytes=48 << 20, collective_id=0, has_side_effects=True),
        name="adjoint",
    )(*arrays)
    return out.reshape(adjoint.shape)


def solution(mesh):
    return jax.shard_map(
        per_device,
        mesh=mesh,
        in_specs=(
            P(None, "blk", "sub", None, None),
            P(None, "blk", "sub", None, None),
            P(None, "blk", "sub", None, None),
            P("blk", None, None, None, None),
            P(("blk", "sub"), None),
            P(("blk", "sub")),
            P(("blk", "sub")),
            P(None, ("blk", "sub")),
        ),
        out_specs=P(None, "blk", "sub", None, None),
        check_vma=False,
    )
```
